512 devices in a mesh: gauss: 128 (over z, x, core), view: 4 (over y).
Axes of the slice: x: 4, y: 4, z: 16, core: 2. Of those that a mesh axis runs over, the one named last changes fastest.
Arguments:
- params: bfloat16 [64, 131072], P(None, 'gauss'), may hold values from -5 to 2, as said below
- lists: int32 [2048, 128], P(('gauss', 'view')), may hold values from -1 to 131071, as said below
- tile_pos: int32 [2048], P(('gauss', 'view')), may hold values from 0 to 255
- cam_index: int32 [2048], P(('gauss', 'view')), may hold values from 0 to 15
- cams: float32 [28, 16], replicated, may hold values from -1 to 1100, as said below
- targets: float32 [3, 2048, 256], P(None, ('gauss', 'view')), may hold values from 0 to 1
Outputs:
- rendered: float32 [3, 2048, 256], P(None, ('gauss', 'view'))
- grads: float32 [64, 131072], P(None, 'gauss')
The draws below stay inside these ranges and needn't reach their ends.
Inputs may be any that keep to these rules, and one draw needn't show every extreme that they name: `lists`: within each tile the entries that are not -1 come first. The entries of one device's 4 tiles that are not -1 name at most 4 times Gaussians of one gauss index (blocks of 1024 consecutive Gaussians), and in every draw some gauss index is named exactly 4 times by the tiles of every device; the number of entries that are not -1 differs from device to device. `cams`: columns are cameras: rows 0-8 a rotation matrix, 9-11 a translation putting every Gaussian mean at depth 2.4 or more, row 12 the focal length, rows 13-27 appearance weights. `params`: rows 6-9 are quaternions whose first component is 1 or more.
All inputs are finite; a program needn't handle non-finite values.
Results may differ from the reference program's by a relative error of at most 0.0003.
Values may be sent and summed in bfloat16 or wider, within the bound.
A program may use at most 64 MiB of HBM per device.

```python
import jax
import jax.numpy as jnp
from jax import lax

G_DEV = 1024
TILES_DEV = 4
LIST = 128
VIEWS = 16
WIN = 16
NG = 131072
TILES = 2048
CAP = 4


def tile_positions(key):
    return jax.random.randint(jax.random.fold_in(key, 7), (TILES,), 0, WIN * WIN).astype(jnp.int32)


def draw_tile_pos(key, part):
    return tile_positions(key)


def draw_params(key, part):
    keys = jax.random.split(key, 8)
    count = NG
    gauss_ids = jnp.arange(count)
    home = gauss_ids % (WIN * WIN)
    home_x = (home % WIN - WIN // 2).astype(jnp.float32)
    home_y = (home // WIN - WIN // 2).astype(jnp.float32)
    offsets = jax.random.uniform(keys[0], (2, count), jnp.float32, 0.0, 16.0)
    mean_z = jax.random.uniform(keys[1], (1, count), jnp.float32, -1.0, 1.0)
    screen_x = 16.0 * home_x[None, :] + offsets[0:1]
    screen_y = 16.0 * home_y[None, :] + offsets[1:2]
    mean_x = screen_x * (4.0 + mean_z) / 1000.0
    mean_y = screen_y * (4.0 + mean_z) / 1000.0
    scales = jax.random.uniform(keys[2], (3, count), jnp.float32, -4.5, -3.0)
    quat_w = jax.random.uniform(keys[3], (1, count), jnp.float32, 1.0, 2.0)
    quat_v = jax.random.uniform(keys[4], (3, count), jnp.float32, -0.5, 0.5)
    opacity = jax.random.uniform(keys[5], (1, count), jnp.float32, -5.0, -2.5)
    shade = jax.random.uniform(keys[6], (48, count), jnp.float32, -0.25, 0.25)
    first = (jnp.arange(48) % 16 == 0).astype(jnp.float32)[:, None]
    shade = shade * (1.0 + first)
    features = jax.random.uniform(keys[7], (5, count), jnp.float32, -0.5, 0.5)
    whole = jnp.concatenate([mean_x, mean_y, mean_z, scales, quat_w, quat_v, opacity, shade, features], axis=0)
    return whole.astype(jnp.bfloat16)


def draw_cams(key, part):
    keys = jax.random.split(key, 5)
    angles = jax.random.uniform(keys[0], (3, VIEWS), jnp.float32, -0.01, 0.01)
    depth = jax.random.uniform(keys[1], (1, VIEWS), jnp.float32, 3.9, 4.1)
    shift_xy = jax.random.uniform(keys[2], (2, VIEWS), jnp.float32, -0.02, 0.02)
    cos_a, sin_a = (jnp.cos(angles[0]), jnp.sin(angles[0]))
    cos_b, sin_b = (jnp.cos(angles[1]), jnp.sin(angles[1]))
    cos_c, sin_c = (jnp.cos(angles[2]), jnp.sin(angles[2]))
    rotation = jnp.stack([cos_b * cos_c, sin_a * sin_b * cos_c - cos_a * sin_c, cos_a * sin_b * cos_c + sin_a * sin_c, cos_b * sin_c, sin_a * sin_b * sin_c + cos_a * cos_c, cos_a * sin_b * sin_c - sin_a * cos_c, -sin_b, sin_a * cos_b, cos_a * cos_b])
    focal = jax.random.uniform(keys[3], (1, VIEWS), jnp.float32, 980.0, 1020.0)
    appear = jax.random.uniform(keys[4], (15, VIEWS), jnp.float32, -0.6, 0.6)
    return jnp.concatenate([rotation, shift_xy, depth, focal, appear], axis=0)


def neighbour_step(step_key, shape):
    pick = jax.random.randint(step_key, shape, 0, 4)
    return jnp.where(pick == 2, -1, jnp.where(pick == 3, 1, 0))


def draw_lists(key, part):
    owners = NG // G_DEV
    blocks = TILES // TILES_DEV
    slots = TILES_DEV * LIST
    per_home = G_DEV // (WIN * WIN)
    hottest = jax.random.randint(jax.random.fold_in(key, 1), (), 0, owners)
    block_positions = tile_positions(key).reshape(blocks, TILES_DEV)

    def one_block(block_key, block_pos):
        keys = jax.random.split(block_key, 7)
        lowest = jax.random.randint(keys[0], (), 0, CAP * 3 // 4 + 1)
        counts = jax.random.randint(keys[1], (owners,), lowest, CAP)
        counts = jnp.where(jnp.arange(owners) == hottest, CAP, counts)
        bounds = jnp.cumsum(counts)
        positions = jnp.arange(slots)
        owner_idx = jnp.searchsorted(bounds, positions, side='right').astype(jnp.int32)
        owner_slots = jnp.where(positions < bounds[-1], owner_idx, -1)
        owner_slots = owner_slots[jax.random.permutation(keys[3], slots)].reshape(TILES_DEV, LIST)
        order = jnp.argsort((owner_slots < 0).astype(jnp.int32), axis=1, stable=True)
        owner_slots = jnp.take_along_axis(owner_slots, order, axis=1)
        near_x = jnp.clip(block_pos[:, None] % WIN + neighbour_step(keys[4], (TILES_DEV, LIST)), 0, WIN - 1)
        near_y = jnp.clip(block_pos[:, None] // WIN + neighbour_step(keys[5], (TILES_DEV, LIST)), 0, WIN - 1)
        layer = jax.random.randint(keys[6], (TILES_DEV, LIST), 0, per_home)
        local_idx = layer * (WIN * WIN) + near_y * WIN + near_x
        return jnp.where(owner_slots >= 0, owner_slots * G_DEV + local_idx, -1)
    block_keys = jax.random.split(jax.random.fold_in(key, 2), blocks)
    return jax.vmap(one_block)(block_keys, block_positions).reshape(TILES, LIST).astype(jnp.int32)


def plant(values, rng, least, high):
    longest = values.shape.index(max(values.shape))
    spots = []
    for shift in (0, 1):
        where = [jax.random.randint(jax.random.fold_in(rng, axis), (), 0, length) for axis, length in enumerate(values.shape)]
        where[longest] = (where[longest] + shift) % values.shape[longest]
        spots.append(tuple(where))
    return values.at[spots[0]].set(least).at[spots[1]].set(high)


def shard_levels(key, dims, pieces, low, high):
    level, own = 1.0, jax.random.fold_in(key, 6)
    for dim, parts in pieces:
        heights = jnp.exp(jax.random.uniform(jax.random.fold_in(own, dim), (parts,), jnp.float32, low / len(pieces), high / len(pieces)))
        level = level * jnp.repeat(heights, dims[dim] // parts).reshape([-1 if axis == dim else 1 for axis in range(len(dims))])
    return level


def setup_inputs(seed: int = 0) -> dict:
    arg_keys = jax.random.split(jax.random.key(seed), 7)
    return {
        "params": draw_params(jax.random.fold_in(arg_keys[6], 71), 0),
        "lists": draw_lists(jax.random.fold_in(arg_keys[6], 71), 0),
        "tile_pos": draw_tile_pos(jax.random.fold_in(arg_keys[6], 71), 0),
        "cam_index": plant(jax.random.randint(arg_keys[3], (TILES,), 0, VIEWS), jax.random.fold_in(arg_keys[3], 1), 0, VIEWS - 1).astype(jnp.int32),
        "cams": draw_cams(jax.random.fold_in(arg_keys[6], 71), 0),
        "targets": jnp.clip(1.0 * jax.random.uniform(arg_keys[5], (3, TILES, 256), jnp.float32) ** shard_levels(arg_keys[5], (3, TILES, 256), ((1, 512),), -0.2, 0.2), 0.0, 1.0),
    }


HIGH = lax.Precision.HIGHEST

def sh_terms(dir_x, dir_y, dir_z):
    return [jnp.ones_like(dir_x), dir_x, dir_y, dir_z, dir_x * dir_y, dir_y * dir_z, dir_x * dir_z, dir_x * dir_x - dir_y * dir_y, 3.0 * dir_z * dir_z - 1.0, dir_x * (dir_x * dir_x - 3.0 * dir_y * dir_y), dir_x * dir_y * dir_z, dir_y * (3.0 * dir_x * dir_x - dir_y * dir_y), dir_z * (dir_x * dir_x - dir_y * dir_y), dir_x * (5.0 * dir_z * dir_z - 1.0), dir_y * (5.0 * dir_z * dir_z - 1.0), dir_z * (5.0 * dir_z * dir_z - 3.0)]

def fix_rows(row_vals, is_live):
    return row_vals.at[6].set(jnp.where(is_live, row_vals[6], 1.0))

def project(row_vals, camcols):
    mean_x, mean_y, mean_z = (row_vals[0], row_vals[1], row_vals[2])
    cam_rot = [camcols[index] for index in range(9)]
    focal = camcols[12]
    cam_x = cam_rot[0] * mean_x + cam_rot[1] * mean_y + cam_rot[2] * mean_z + camcols[9]
    cam_y = cam_rot[3] * mean_x + cam_rot[4] * mean_y + cam_rot[5] * mean_z + camcols[10]
    cam_z = cam_rot[6] * mean_x + cam_rot[7] * mean_y + cam_rot[8] * mean_z + camcols[11]
    inv_z = 1.0 / cam_z
    quaternion = row_vals[6:10]
    q_norm = jnp.sqrt(lax.optimization_barrier(jnp.sum(quaternion * quaternion, axis=0)))
    unit_w = quaternion[0] / q_norm
    unit_x = quaternion[1] / q_norm
    unit_y = quaternion[2] / q_norm
    unit_z = quaternion[3] / q_norm
    rotation = [[1.0 - 2.0 * (unit_y * unit_y + unit_z * unit_z), 2.0 * (unit_x * unit_y - unit_w * unit_z), 2.0 * (unit_x * unit_z + unit_w * unit_y)], [2.0 * (unit_x * unit_y + unit_w * unit_z), 1.0 - 2.0 * (unit_x * unit_x + unit_z * unit_z), 2.0 * (unit_y * unit_z - unit_w * unit_x)], [2.0 * (unit_x * unit_z - unit_w * unit_y), 2.0 * (unit_y * unit_z + unit_w * unit_x), 1.0 - 2.0 * (unit_x * unit_x + unit_y * unit_y)]]
    mixed = [[cam_rot[3 * row_i] * rotation[0][col_k] + cam_rot[3 * row_i + 1] * rotation[1][col_k] + cam_rot[3 * row_i + 2] * rotation[2][col_k] for col_k in range(3)] for row_i in range(3)]
    jac_scale = focal * inv_z
    proj_u = [jac_scale * mixed[0][col_k] - jac_scale * cam_x * inv_z * mixed[2][col_k] for col_k in range(3)]
    proj_v = [jac_scale * mixed[1][col_k] - jac_scale * cam_y * inv_z * mixed[2][col_k] for col_k in range(3)]
    var_diag = jnp.exp(2.0 * row_vals[3:6])
    cov_a = proj_u[0] * proj_u[0] * var_diag[0] + proj_u[1] * proj_u[1] * var_diag[1] + proj_u[2] * proj_u[2] * var_diag[2] + 0.3
    cov_b = proj_u[0] * proj_v[0] * var_diag[0] + proj_u[1] * proj_v[1] * var_diag[1] + proj_u[2] * proj_v[2] * var_diag[2]
    cov_c = proj_v[0] * proj_v[0] * var_diag[0] + proj_v[1] * proj_v[1] * var_diag[1] + proj_v[2] * proj_v[2] * var_diag[2] + 0.3
    determinant = cov_a * cov_c - cov_b * cov_b
    opacity = jax.nn.sigmoid(row_vals[10])
    distance = jnp.sqrt(cam_x * cam_x + cam_y * cam_y + cam_z * cam_z)
    terms = sh_terms(cam_x / distance, cam_y / distance, cam_z / distance)
    colors = []
    for chan in range(3):
        shade = 0.5 + sum((row_vals[11 + 16 * chan + basis_b] * terms[basis_b] for basis_b in range(16)))
        shade = shade + sum((row_vals[59 + feat_j] * camcols[13 + 3 * feat_j + chan] for feat_j in range(5)))
        colors.append(shade)
    centre_u = focal * cam_x * inv_z
    centre_v = focal * cam_y * inv_z
    return jnp.stack([centre_u, centre_v, cov_c / determinant, -cov_b / determinant, cov_a / determinant, opacity, colors[0], colors[1], colors[2]])

def render(attrs, is_live, pixel_x, pixel_y):
    diff_x = pixel_x[None, :] - attrs[0][:, None]
    diff_y = pixel_y[None, :] - attrs[1][:, None]
    power = -0.5 * (attrs[2][:, None] * diff_x * diff_x + 2.0 * attrs[3][:, None] * diff_x * diff_y + attrs[4][:, None] * diff_y * diff_y)
    alpha = jnp.where(is_live[:, None], attrs[5][:, None] * jnp.exp(power), 0.0)
    keeping = jnp.cumprod(1.0 - alpha, axis=0)
    transmit = jnp.concatenate([jnp.ones((1, alpha.shape[1]), alpha.dtype), keeping[:-1]], axis=0)
    return jnp.dot(attrs[6:9], alpha * transmit, precision=HIGH)

def pixels(position):
    pixel_idx = jnp.arange(256)
    pixel_x = (16 * (position % WIN - WIN // 2) + pixel_idx % 16).astype(jnp.float32) + 0.5
    pixel_y = (16 * (position // WIN - WIN // 2) + pixel_idx // 16).astype(jnp.float32) + 0.5
    return (pixel_x, pixel_y)

def tile_grads(row_vals, camcol, is_live, pixel_x, pixel_y, target):

    def loss_of(params_in):
        picture = render(project(params_in, camcol[:, None]), is_live, pixel_x, pixel_y)
        return (0.5 * jnp.sum((picture - target) ** 2), picture)
    loss_val, pullback, picture = jax.vjp(loss_of, row_vals, has_aux=True)
    return (picture, pullback(jnp.ones_like(loss_val))[0])

def reference(params, lists, tile_pos, cam_index, cams, targets):
    num_gauss = params.shape[1]

    def one_tile(packed):
        ids, position, camera, target = packed
        is_live = ids >= 0
        row_vals = fix_rows(params[:, jnp.maximum(ids, 0)].astype(jnp.float32), is_live)
        camcol = cams[:, camera]
        pixel_x, pixel_y = pixels(position)
        return tile_grads(row_vals, camcol, is_live, pixel_x, pixel_y, target)
    pictures, tile_g = lax.map(one_tile, (lists, tile_pos, cam_index, jnp.transpose(targets, (1, 0, 2))), batch_size=64)
    flat_ids = jnp.where(lists >= 0, lists, num_gauss).reshape(-1)
    slot_g = jnp.transpose(tile_g, (1, 0, 2)).reshape(params.shape[0], -1)
    summed = jnp.zeros((params.shape[0], num_gauss), jnp.float32).at[:, flat_ids].add(slot_g, mode='drop')
    return (jnp.transpose(pictures, (1, 0, 2)), summed)
```

```python
import jax
import jax.numpy as jnp
from jax import lax
from jax.experimental import pallas as pl
from jax.experimental.pallas import tpu as pltpu
from jax.sharding import PartitionSpec as P

WIN = 16


def sh_terms(dir_x, dir_y, dir_z):
    return [
        jnp.ones_like(dir_x),
        dir_x,
        dir_y,
        dir_z,
        dir_x * dir_y,
        dir_y * dir_z,
        dir_x * dir_z,
        dir_x * dir_x - dir_y * dir_y,
        3.0 * dir_z * dir_z - 1.0,
        dir_x * (dir_x * dir_x - 3.0 * dir_y * dir_y),
        dir_x * dir_y * dir_z,
        dir_y * (3.0 * dir_x * dir_x - dir_y * dir_y),
        dir_z * (dir_x * dir_x - dir_y * dir_y),
        dir_x * (5.0 * dir_z * dir_z - 1.0),
        dir_y * (5.0 * dir_z * dir_z - 1.0),
        dir_z * (5.0 * dir_z * dir_z - 3.0),
    ]


def project(row_vals, camcols):
    mean_x, mean_y, mean_z = (row_vals[0], row_vals[1], row_vals[2])
    cam_rot = [camcols[index] for index in range(9)]
    focal = camcols[12]
    cam_x = cam_rot[0] * mean_x + cam_rot[1] * mean_y + cam_rot[2] * mean_z + camcols[9]
    cam_y = cam_rot[3] * mean_x + cam_rot[4] * mean_y + cam_rot[5] * mean_z + camcols[10]
    cam_z = cam_rot[6] * mean_x + cam_rot[7] * mean_y + cam_rot[8] * mean_z + camcols[11]
    inv_z = 1.0 / cam_z
    quaternion = row_vals[6:10]
    q_norm = jnp.sqrt(
        quaternion[0] * quaternion[0]
        + quaternion[1] * quaternion[1]
        + quaternion[2] * quaternion[2]
        + quaternion[3] * quaternion[3]
    )
    unit_w = quaternion[0] / q_norm
    unit_x = quaternion[1] / q_norm
    unit_y = quaternion[2] / q_norm
    unit_z = quaternion[3] / q_norm
    rotation = [
        [
            1.0 - 2.0 * (unit_y * unit_y + unit_z * unit_z),
            2.0 * (unit_x * unit_y - unit_w * unit_z),
            2.0 * (unit_x * unit_z + unit_w * unit_y),
        ],
        [
            2.0 * (unit_x * unit_y + unit_w * unit_z),
            1.0 - 2.0 * (unit_x * unit_x + unit_z * unit_z),
            2.0 * (unit_y * unit_z - unit_w * unit_x),
        ],
        [
            2.0 * (unit_x * unit_z - unit_w * unit_y),
            2.0 * (unit_y * unit_z + unit_w * unit_x),
            1.0 - 2.0 * (unit_x * unit_x + unit_y * unit_y),
        ],
    ]
    mixed = [
        [
            cam_rot[3 * row_i] * rotation[0][col_k]
            + cam_rot[3 * row_i + 1] * rotation[1][col_k]
            + cam_rot[3 * row_i + 2] * rotation[2][col_k]
            for col_k in range(3)
        ]
        for row_i in range(3)
    ]
    jac_scale = focal * inv_z
    proj_u = [
        jac_scale * mixed[0][col_k] - jac_scale * cam_x * inv_z * mixed[2][col_k]
        for col_k in range(3)
    ]
    proj_v = [
        jac_scale * mixed[1][col_k] - jac_scale * cam_y * inv_z * mixed[2][col_k]
        for col_k in range(3)
    ]
    var_diag = [jnp.exp(2.0 * row_vals[axis]) for axis in range(3, 6)]
    cov_a = (
        proj_u[0] * proj_u[0] * var_diag[0]
        + proj_u[1] * proj_u[1] * var_diag[1]
        + proj_u[2] * proj_u[2] * var_diag[2]
        + 0.3
    )
    cov_b = (
        proj_u[0] * proj_v[0] * var_diag[0]
        + proj_u[1] * proj_v[1] * var_diag[1]
        + proj_u[2] * proj_v[2] * var_diag[2]
    )
    cov_c = (
        proj_v[0] * proj_v[0] * var_diag[0]
        + proj_v[1] * proj_v[1] * var_diag[1]
        + proj_v[2] * proj_v[2] * var_diag[2]
        + 0.3
    )
    determinant = cov_a * cov_c - cov_b * cov_b
    opacity = jax.nn.sigmoid(row_vals[10])
    distance = jnp.sqrt(cam_x * cam_x + cam_y * cam_y + cam_z * cam_z)
    terms = sh_terms(cam_x / distance, cam_y / distance, cam_z / distance)
    colors = []
    for chan in range(3):
        shade = 0.5 + sum(
            (row_vals[11 + 16 * chan + basis_b] * terms[basis_b] for basis_b in range(16))
        )
        shade = shade + sum(
            (row_vals[59 + feat_j] * camcols[13 + 3 * feat_j + chan] for feat_j in range(5))
        )
        colors.append(shade)
    centre_u = focal * cam_x * inv_z
    centre_v = focal * cam_y * inv_z
    return [
        centre_u,
            centre_v,
            cov_c / determinant,
            -cov_b / determinant,
            cov_a / determinant,
            opacity,
            colors[0],
            colors[1],
            colors[2],
    ]


def tile_values(scalars, shape):
    tile = lax.broadcasted_iota(jnp.int32, shape, 0) % len(scalars)
    out = jnp.full(shape, scalars[0])
    for index, value in enumerate(scalars[1:], 1):
        out = jnp.where(tile == index, value, out)
    return out


def render_kernel(
    rows_ref, ids_ref, pos_ref, cam_ref, cams_ref, target_ref,
    picture_ref, grads_ref,
    dx_s, dy_s, exp_s, alpha_s, trans_s, color_s,
):
    n_tiles, slots = ids_ref.shape
    half = target_ref.shape[2] // 2
    wide = (2 * n_tiles, half)
    narrow = (n_tiles, slots)
    live = ids_ref[...] >= 0
    camcols = [
        tile_values([cams_ref[row, cam_ref[t]] for t in range(n_tiles)], narrow)
        for row in range(cams_ref.shape[0])
    ]
    row_vals = [rows_ref[row].astype(jnp.float32) for row in range(rows_ref.shape[0])]
    row_vals[6] = jnp.where(live, row_vals[6], 1.0)
    attrs, pullback = jax.vjp(lambda vals: project(vals, camcols), row_vals)
    attrs_live = list(attrs)
    for index in range(2, 6):
        attrs_live[index] = jnp.where(live, attrs[index], 0.0)
    attrs8 = [jnp.concatenate([a, a], axis=0) for a in attrs_live]

    row_id = lax.broadcasted_iota(jnp.int32, wide, 0)
    lane = lax.broadcasted_iota(jnp.int32, wide, 1)
    pixel = lane + jnp.where(row_id >= n_tiles, half, 0)
    base_x = tile_values([16 * (pos_ref[t] % WIN - WIN // 2) for t in range(n_tiles)], wide)
    base_y = tile_values([16 * (pos_ref[t] // WIN - WIN // 2) for t in range(n_tiles)], wide)
    pixel_x = (base_x + pixel % 16).astype(jnp.float32) + 0.5
    pixel_y = (base_y + pixel // 16).astype(jnp.float32) + 0.5

    def spread(values, slot):
        at = jnp.full(wide, slot, jnp.int32)
        return jnp.take_along_axis(values, at, axis=1, mode="promise_in_bounds")

    unroll = 8

    def forward(step, carry):
        trans, r0, r1, r2 = carry
        for inner in range(unroll):
            slot = step * unroll + inner
            u, v, ca, cb, cc, op, c0, c1, c2 = [spread(a, slot) for a in attrs8]
            dx = pixel_x - u
            dy = pixel_y - v
            power = -0.5 * (ca * dx * dx + 2.0 * cb * dx * dy + cc * dy * dy)
            e = jnp.exp(power)
            alpha = op * e
            dx_s[slot] = dx
            dy_s[slot] = dy
            exp_s[slot] = e
            alpha_s[slot] = alpha
            trans_s[slot] = trans
            color_s[0, slot] = c0
            color_s[1, slot] = c1
            color_s[2, slot] = c2
            w = alpha * trans
            r0, r1, r2 = r0 + c0 * w, r1 + c1 * w, r2 + c2 * w
            trans = trans * (1.0 - alpha)
        return trans, r0, r1, r2

    zero = jnp.zeros(wide, jnp.float32)
    _, r0, r1, r2 = lax.fori_loop(
        0, slots // unroll, forward, (jnp.ones(wide, jnp.float32), zero, zero, zero)
    )
    res = []
    for chan, pic in enumerate((r0, r1, r2)):
        picture_ref[chan, :, :half] = pic[:n_tiles]
        picture_ref[chan, :, half:] = pic[n_tiles:]
        want = target_ref[chan]
        res.append(pic - jnp.concatenate([want[:, :half], want[:, half:]], axis=0))

    def backward(step, carry):
        behind, accs = carry
        accs = list(accs)
        for inner in range(unroll):
            slot = slots - 1 - (step * unroll + inner)
            dx, dy, e, alpha, trans = dx_s[slot], dy_s[slot], exp_s[slot], alpha_s[slot], trans_s[slot]
            q = color_s[0, slot] * res[0] + color_s[1, slot] * res[1] + color_s[2, slot] * res[2]
            w = alpha * trans
            diff = q - behind
            gain = trans * diff * e
            behind = behind + alpha * diff
            gx = gain * dx
            gy = gain * dy
            terms = [gain, gx, gy, gx * dx, gx * dy, gy * dy, w * res[0], w * res[1], w * res[2]]
            here = lane == slot
            for index, term in enumerate(terms):
                total = jnp.sum(term, axis=1, keepdims=True)
                accs[index] = jnp.where(here, total, accs[index])
        return behind, tuple(accs)

    _, accs = lax.fori_loop(0, slots // unroll, backward, (zero, (zero,) * 9))
    g0, gx, gy, gxx, gxy, gyy, k0, k1, k2 = [a[:n_tiles] + a[n_tiles:] for a in accs]
    op = attrs_live[5]
    ca, cb, cc = attrs_live[2:5]
    cot = [
        op * (ca * gx + cb * gy),
        op * (cb * gx + cc * gy),
        -0.5 * (op * gxx),
        -(op * gxy),
        -0.5 * (op * gyy),
        g0,
        k0,
        k1,
        k2,
    ]
    cot = [jnp.where(live, value, 0.0) for value in cot]
    (grads,) = pullback(cot)
    for row, value in enumerate(grads):
        grads_ref[row] = value


def render_call(rows, lists, tile_pos, cam_index, cams, targets, interpret=False):
    width = rows.shape[0]
    n_tiles, slots = lists.shape
    lanes = targets.shape[2] // 2
    vmem = pl.BlockSpec(memory_space=pltpu.VMEM)
    smem = pl.BlockSpec(memory_space=pltpu.SMEM)
    plane = pltpu.VMEM((slots, 2 * n_tiles, lanes), jnp.float32)
    return pl.pallas_call(
        render_kernel,
        out_shape=(
            jax.ShapeDtypeStruct(targets.shape, jnp.float32),
            jax.ShapeDtypeStruct((width, n_tiles, slots), jnp.float32),
        ),
        in_specs=[vmem, vmem, smem, smem, smem, vmem],
        out_specs=(vmem, vmem),
        scratch_shapes=[plane] * 5
        + [pltpu.VMEM((3, slots, 2 * n_tiles, lanes), jnp.float32)],
        interpret=interpret,
    )(rows, lists, tile_pos, cam_index, cams, targets)


def reduce_kernel(n_view, idx_ref, rows_ref, out_ref, local, arrived, gathered, sem_a, sem_b):
    me = lax.axis_index("view")
    width, g_dev = out_ref.shape
    chunk = width // n_view
    barrier = pltpu.get_barrier_semaphore()
    for step in range(1, n_view):
        pl.semaphore_signal(
            barrier,
            inc=1,
            device_id={"view": lax.rem(me + step, n_view)},
            device_id_type=pl.DeviceIdType.MESH,
        )
    n_idx = idx_ref.shape[1]
    hot = jnp.where(
        lax.broadcasted_iota(jnp.int32, (g_dev, n_idx), 0) == idx_ref[...], 1.0, 0.0
    ).astype(jnp.bfloat16)
    rest = rows_ref[...]
    total = jnp.zeros((width, g_dev), jnp.float32)
    for _ in range(3):
        piece = rest.astype(jnp.bfloat16)
        rest = rest - piece.astype(jnp.float32)
        total = total + lax.dot_general(
            piece, hot, (((1,), (1,)), ((), ())), preferred_element_type=jnp.float32
        )
    local[...] = total.reshape(n_view, chunk, g_dev)
    pl.semaphore_wait(barrier, n_view - 1)
    first = []
    for step in range(1, n_view):
        peer = lax.rem(me + step, n_view)
        copy = pltpu.make_async_remote_copy(
            src_ref=local.at[peer],
            dst_ref=arrived.at[step - 1],
            send_sem=sem_a.at[0, step - 1],
            recv_sem=sem_a.at[1, step - 1],
            device_id={"view": peer},
            device_id_type=pl.DeviceIdType.MESH,
        )
        copy.start()
        first.append(copy)
    for copy in first:
        copy.wait()
    mine = local[me]
    for step in range(1, n_view):
        mine = mine + arrived[step - 1]
    gathered[0] = mine
    second = []
    for step in range(1, n_view):
        peer = lax.rem(me + step, n_view)
        copy = pltpu.make_async_remote_copy(
            src_ref=gathered.at[0],
            dst_ref=gathered.at[step],
            send_sem=sem_b.at[0, step - 1],
            recv_sem=sem_b.at[1, step - 1],
            device_id={"view": peer},
            device_id_type=pl.DeviceIdType.MESH,
        )
        copy.start()
        second.append(copy)
    for copy in second:
        copy.wait()
    for step in range(n_view):
        origin = lax.rem(me + n_view - step, n_view)
        out_ref[pl.ds(pl.multiple_of(origin * chunk, chunk), chunk)] = gathered[step]


def reduce_call(idx, rows, g_dev):
    n_view = lax.axis_size("view")
    width = rows.shape[0]
    chunk = width // n_view
    vmem = pl.BlockSpec(memory_space=pltpu.VMEM)
    return pl.pallas_call(
        lambda *refs: reduce_kernel(n_view, *refs),
        out_shape=jax.ShapeDtypeStruct((width, g_dev), jnp.float32),
        in_specs=[vmem, vmem],
        out_specs=vmem,
        scratch_shapes=[
            pltpu.VMEM((n_view, chunk, g_dev), jnp.float32),
            pltpu.VMEM((n_view - 1, chunk, g_dev), jnp.float32),
            pltpu.VMEM((n_view, chunk, g_dev), jnp.float32),
            pltpu.SemaphoreType.DMA((2, n_view - 1)),
            pltpu.SemaphoreType.DMA((2, n_view - 1)),
        ],
        compiler_params=pltpu.CompilerParams(collective_id=0, has_side_effects=True),
    )(idx, rows)


def on_device(params, lists, tile_pos, cam_index, cams, targets):
    owners = lax.axis_size("gauss")
    g_dev = params.shape[1]
    width = params.shape[0]
    n_tiles, list_len = lists.shape
    capacity = n_tiles * list_len // owners
    flat_ids = lists.reshape(-1)
    is_live = flat_ids >= 0
    owner_idx = jnp.where(is_live, flat_ids // g_dev, owners)
    selector = (owner_idx[:, None] == jnp.arange(owners)[None, :]).astype(jnp.int32)
    ranks = jnp.sum((jnp.cumsum(selector, axis=0) - selector) * selector, axis=1)
    slot_pos = jnp.where(is_live, owner_idx * capacity + ranks, owners * capacity)
    read_pos = jnp.minimum(slot_pos, owners * capacity - 1)
    local_idx = jnp.where(is_live, flat_ids % g_dev, -1)
    wanted = (
        jnp.full((owners * capacity,), -1, jnp.int32)
        .at[slot_pos]
        .set(local_idx, mode="drop")
        .reshape(owners, capacity)
    )
    received = lax.all_to_all(wanted, "gauss", split_axis=0, concat_axis=0, tiled=True).reshape(-1)
    picked = jnp.take(params, jnp.maximum(received, 0), axis=1)
    returned = lax.all_to_all(
        picked.reshape(width, owners, capacity), "gauss", split_axis=1, concat_axis=1, tiled=True
    )
    slot_rows = jnp.take(returned.reshape(width, -1), read_pos, axis=1).reshape(
        width, n_tiles, list_len
    )
    pictures, tile_g = render_call(slot_rows, lists, tile_pos, cam_index, cams, targets)
    slot_g = tile_g.reshape(width, -1)
    sent_g = (
        jnp.zeros((width, owners * capacity), jnp.float32).at[:, slot_pos].set(slot_g, mode="drop")
    )
    row_g = lax.all_to_all(
        sent_g.reshape(width, owners, capacity), "gauss", split_axis=1, concat_axis=1, tiled=True
    ).reshape(width, -1)
    grads = reduce_call(received.reshape(1, -1), row_g, g_dev)
    return (pictures, grads)


def solution(mesh):
    return jax.shard_map(
        on_device,
        mesh=mesh,
        in_specs=(
            P(None, "gauss"),
            P(("gauss", "view"), None),
            P(("gauss", "view")),
            P(("gauss", "view")),
            P(),
            P(None, ("gauss", "view"), None),
        ),
        out_specs=(P(None, ("gauss", "view"), None), P(None, "gauss")),
        check_vma=False,
    )
```

```python
import jax
import jax.numpy as jnp
from jax import lax
from jax.experimental import pallas as pl
from jax.experimental.pallas import tpu as pltpu
from jax.sharding import PartitionSpec as P

WIN = 16


def sh_terms(dir_x, dir_y, dir_z):
    return [
        jnp.ones_like(dir_x),
        dir_x,
        dir_y,
        dir_z,
        dir_x * dir_y,
        dir_y * dir_z,
        dir_x * dir_z,
        dir_x * dir_x - dir_y * dir_y,
        3.0 * dir_z * dir_z - 1.0,
        dir_x * (dir_x * dir_x - 3.0 * dir_y * dir_y),
        dir_x * dir_y * dir_z,
        dir_y * (3.0 * dir_x * dir_x - dir_y * dir_y),
        dir_z * (dir_x * dir_x - dir_y * dir_y),
        dir_x * (5.0 * dir_z * dir_z - 1.0),
        dir_y * (5.0 * dir_z * dir_z - 1.0),
        dir_z * (5.0 * dir_z * dir_z - 3.0),
    ]


def project(row_vals, camcols):
    mean_x, mean_y, mean_z = (row_vals[0], row_vals[1], row_vals[2])
    cam_rot = [camcols[index] for index in range(9)]
    focal = camcols[12]
    cam_x = cam_rot[0] * mean_x + cam_rot[1] * mean_y + cam_rot[2] * mean_z + camcols[9]
    cam_y = cam_rot[3] * mean_x + cam_rot[4] * mean_y + cam_rot[5] * mean_z + camcols[10]
    cam_z = cam_rot[6] * mean_x + cam_rot[7] * mean_y + cam_rot[8] * mean_z + camcols[11]
    inv_z = 1.0 / cam_z
    quaternion = row_vals[6:10]
    q_norm = jnp.sqrt(
        quaternion[0] * quaternion[0]
        + quaternion[1] * quaternion[1]
        + quaternion[2] * quaternion[2]
        + quaternion[3] * quaternion[3]
    )
    unit_w = quaternion[0] / q_norm
    unit_x = quaternion[1] / q_norm
    unit_y = quaternion[2] / q_norm
    unit_z = quaternion[3] / q_norm
    rotation = [
        [
            1.0 - 2.0 * (unit_y * unit_y + unit_z * unit_z),
            2.0 * (unit_x * unit_y - unit_w * unit_z),
            2.0 * (unit_x * unit_z + unit_w * unit_y),
        ],
        [
            2.0 * (unit_x * unit_y + unit_w * unit_z),
            1.0 - 2.0 * (unit_x * unit_x + unit_z * unit_z),
            2.0 * (unit_y * unit_z - unit_w * unit_x),
        ],
        [
            2.0 * (unit_x * unit_z - unit_w * unit_y),
            2.0 * (unit_y * unit_z + unit_w * unit_x),
            1.0 - 2.0 * (unit_x * unit_x + unit_y * unit_y),
        ],
    ]
    mixed = [
        [
            cam_rot[3 * row_i] * rotation[0][col_k]
            + cam_rot[3 * row_i + 1] * rotation[1][col_k]
            + cam_rot[3 * row_i + 2] * rotation[2][col_k]
            for col_k in range(3)
        ]
        for row_i in range(3)
    ]
    jac_scale = focal * inv_z
    proj_u = [
        jac_scale * mixed[0][col_k] - jac_scale * cam_x * inv_z * mixed[2][col_k]
        for col_k in range(3)
    ]
    proj_v = [
        jac_scale * mixed[1][col_k] - jac_scale * cam_y * inv_z * mixed[2][col_k]
        for col_k in range(3)
    ]
    var_diag = [jnp.exp(2.0 * row_vals[axis]) for axis in range(3, 6)]
    cov_a = (
        proj_u[0] * proj_u[0] * var_diag[0]
        + proj_u[1] * proj_u[1] * var_diag[1]
        + proj_u[2] * proj_u[2] * var_diag[2]
        + 0.3
    )
    cov_b = (
        proj_u[0] * proj_v[0] * var_diag[0]
        + proj_u[1] * proj_v[1] * var_diag[1]
        + proj_u[2] * proj_v[2] * var_diag[2]
    )
    cov_c = (
        proj_v[0] * proj_v[0] * var_diag[0]
        + proj_v[1] * proj_v[1] * var_diag[1]
        + proj_v[2] * proj_v[2] * var_diag[2]
        + 0.3
    )
    determinant = cov_a * cov_c - cov_b * cov_b
    opacity = jax.nn.sigmoid(row_vals[10])
    distance = jnp.sqrt(cam_x * cam_x + cam_y * cam_y + cam_z * cam_z)
    terms = sh_terms(cam_x / distance, cam_y / distance, cam_z / distance)
    colors = []
    for chan in range(3):
        shade = 0.5 + sum(
            (row_vals[11 + 16 * chan + basis_b] * terms[basis_b] for basis_b in range(16))
        )
        shade = shade + sum(
            (row_vals[59 + feat_j] * camcols[13 + 3 * feat_j + chan] for feat_j in range(5))
        )
        colors.append(shade)
    centre_u = focal * cam_x * inv_z
    centre_v = focal * cam_y * inv_z
    return [
        centre_u,
            centre_v,
            cov_c / determinant,
            -cov_b / determinant,
            cov_a / determinant,
            opacity,
            colors[0],
            colors[1],
            colors[2],
    ]


def tile_values(scalars, shape):
    tile = lax.broadcasted_iota(jnp.int32, shape, 0) % len(scalars)
    out = jnp.full(shape, scalars[0])
    for index, value in enumerate(scalars[1:], 1):
        out = jnp.where(tile == index, value, out)
    return out


def render_tiles(
    rows_ref, ids_ref, pos_ref, cam_ref, cams_ref, target_ref, picture_ref,
    dx_s, dy_s, exp_s, alpha_s, trans_s, color_s,
):
    n_tiles, slots = ids_ref.shape
    half = target_ref.shape[2] // 2
    wide = (2 * n_tiles, half)
    narrow = (n_tiles, slots)
    live = ids_ref[...] >= 0
    camcols = [
        tile_values([cams_ref[row, cam_ref[t]] for t in range(n_tiles)], narrow)
        for row in range(cams_ref.shape[0])
    ]
    row_vals = [rows_ref[row] for row in range(rows_ref.shape[0])]
    row_vals[6] = jnp.where(live, row_vals[6], 1.0)
    attrs, pullback = jax.vjp(lambda vals: project(vals, camcols), row_vals)
    attrs_live = list(attrs)
    for index in range(9):
        attrs_live[index] = jnp.where(live, attrs[index], 0.0)
    attrs8 = [jnp.concatenate([a, a], axis=0) for a in attrs_live]

    row_id = lax.broadcasted_iota(jnp.int32, wide, 0)
    lane = lax.broadcasted_iota(jnp.int32, wide, 1)
    pixel = lane + jnp.where(row_id >= n_tiles, half, 0)
    base_x = tile_values([16 * (pos_ref[t] % WIN - WIN // 2) for t in range(n_tiles)], wide)
    base_y = tile_values([16 * (pos_ref[t] // WIN - WIN // 2) for t in range(n_tiles)], wide)
    pixel_x = (base_x + pixel % 16).astype(jnp.float32) + 0.5
    pixel_y = (base_y + pixel // 16).astype(jnp.float32) + 0.5

    def spread(values, slot):
        at = jnp.full(wide, slot, jnp.int32)
        return jnp.take_along_axis(values, at, axis=1, mode="promise_in_bounds")

    unroll = 8

    def forward(step, carry):
        trans, r0, r1, r2 = carry
        for inner in range(unroll):
            slot = step * unroll + inner
            u, v, ca, cb, cc, op, c0, c1, c2 = [spread(a, slot) for a in attrs8]
            dx = pixel_x - u
            dy = pixel_y - v
            power = -0.5 * (ca * dx * dx + 2.0 * cb * dx * dy + cc * dy * dy)
            e = jnp.exp(power)
            alpha = op * e
            dx_s[slot] = dx
            dy_s[slot] = dy
            exp_s[slot] = e
            alpha_s[slot] = alpha
            trans_s[slot] = trans
            color_s[0, slot] = c0
            color_s[1, slot] = c1
            color_s[2, slot] = c2
            w = alpha * trans
            r0, r1, r2 = r0 + c0 * w, r1 + c1 * w, r2 + c2 * w
            trans = trans * (1.0 - alpha)
        return trans, r0, r1, r2

    zero = jnp.zeros(wide, jnp.float32)
    _, r0, r1, r2 = lax.fori_loop(
        0, slots // unroll, forward, (jnp.ones(wide, jnp.float32), zero, zero, zero)
    )
    res = []
    for chan, pic in enumerate((r0, r1, r2)):
        picture_ref[chan, :, :half] = pic[:n_tiles]
        picture_ref[chan, :, half:] = pic[n_tiles:]
        want = target_ref[chan]
        res.append(pic - jnp.concatenate([want[:, :half], want[:, half:]], axis=0))

    def backward(step, carry):
        behind, accs = carry
        accs = list(accs)
        for inner in range(unroll):
            slot = slots - 1 - (step * unroll + inner)
            dx, dy, e, alpha, trans = dx_s[slot], dy_s[slot], exp_s[slot], alpha_s[slot], trans_s[slot]
            q = color_s[0, slot] * res[0] + color_s[1, slot] * res[1] + color_s[2, slot] * res[2]
            w = alpha * trans
            diff = q - behind
            gain = trans * diff * e
            behind = behind + alpha * diff
            gx = gain * dx
            gy = gain * dy
            terms = [gain, gx, gy, gx * dx, gx * dy, gy * dy, w * res[0], w * res[1], w * res[2]]
            here = lane == slot
            for index, term in enumerate(terms):
                total = jnp.sum(term, axis=1, keepdims=True)
                accs[index] = jnp.where(here, total, accs[index])
        return behind, tuple(accs)

    _, accs = lax.fori_loop(0, slots // unroll, backward, (zero, (zero,) * 9))
    g0, gx, gy, gxx, gxy, gyy, k0, k1, k2 = [a[:n_tiles] + a[n_tiles:] for a in accs]
    op = attrs_live[5]
    ca, cb, cc = attrs_live[2:5]
    cot = [
        op * (ca * gx + cb * gy),
        op * (cb * gx + cc * gy),
        -0.5 * (op * gxx),
        -(op * gxy),
        -0.5 * (op * gyy),
        g0,
        k0,
        k1,
        k2,
    ]
    cot = [jnp.where(live, value, 0.0) for value in cot]
    (grads,) = pullback(cot)
    for row, value in enumerate(grads):
        rows_ref[row] = jnp.where(live, value, 0.0)


CAP = 4


def pieces(values):
    out = []
    for _ in range(3):
        out.append(values.astype(jnp.bfloat16))
        values = values - out[-1].astype(jnp.float32)
    return out


def dot(a, b, dims):
    return lax.dot_general(a, b, (dims, ((), ())), preferred_element_type=jnp.float32)


def step_kernel(
    n_view, n_z, n_c,
    params_ref, ids_ref, pos_ref, cam_ref, cams_ref, target_ref,
    picture_ref, out_ref,
    want_s, ask_a, ask_b, par_x, par_y, par_s, par_q, rows_s,
    grad_s, grad_y, grad_x, grad_u, hot_s, pick_s,
    dx_s, dy_s, exp_s, alpha_s, trans_s, color_s,
    local, arrived, gathered,
    sem_z, sem_c, sem_v,
):
    owners = n_z * n_c
    width, g_dev = params_ref.shape
    n_tiles, slots = ids_ref.shape
    f32, bf16 = jnp.float32, jnp.bfloat16
    me = lax.axis_index("gauss")
    my_view = lax.axis_index("view")
    my_z, my_c = me // n_c, lax.rem(me, n_c)

    def z_peer(step):
        other = lax.rem(my_z + step, n_z)
        return other, {"gauss": other * n_c + my_c}

    def c_peer(step):
        other = lax.rem(my_c + step, n_c)
        return other, {"gauss": my_z * n_c + other}

    def v_peer(step):
        other = lax.rem(my_view + step, n_view)
        return other, {"view": other}

    barrier = pltpu.get_barrier_semaphore()
    for count, peer in ((n_z, z_peer), (n_c, c_peer), (n_view, v_peer)):
        for step in range(1, count):
            pl.semaphore_signal(
                barrier, inc=1, device_id=peer(step)[1], device_id_type=pl.DeviceIdType.MESH
            )

    def exchange(count, peer, sems, phase, source, target):
        copies = []
        for step in range(1, count):
            other, device = peer(step)
            copy = pltpu.make_async_remote_copy(
                src_ref=source(other),
                dst_ref=target(step),
                send_sem=sems.at[phase, 0, step - 1],
                recv_sem=sems.at[phase, 1, step - 1],
                device_id=device,
                device_id_type=pl.DeviceIdType.MESH,
            )
            copy.start()
            copies.append(copy)
        return copies

    def finish(copies):
        for copy in copies:
            copy.wait()

    bits = g_dev.bit_length() - 1
    own_row = lax.broadcasted_iota(jnp.int32, (owners, slots), 0)
    lane = lax.broadcasted_iota(jnp.int32, (owners, slots), 1)
    before = (
        lax.broadcasted_iota(jnp.int32, (slots, slots), 0)
        < lax.broadcasted_iota(jnp.int32, (slots, slots), 1)
    )
    before = jnp.where(before, 1.0, 0.0).astype(bf16)
    seen = jnp.zeros((owners, 1), f32)
    asked = [jnp.zeros((owners, slots), f32) for _ in range(CAP)]
    for t in range(n_tiles):
        ids = ids_ref[t : t + 1, :]
        owner = lax.shift_right_arithmetic(ids, bits)
        index = (lax.bitwise_and(ids, g_dev - 1) + 1).astype(f32)
        named = own_row == owner
        named_f = jnp.where(named, 1.0, 0.0)
        rank = dot(named_f.astype(bf16), before, ((1,), (0,))) + seen
        seen = seen + jnp.sum(named_f, axis=1, keepdims=True)
        for c in range(CAP):
            chosen = jnp.where(rank == float(c), named_f, 0.0)
            pick_s[c, :, t * slots : (t + 1) * slots] = chosen.astype(bf16)
            asked[c] = asked[c] + chosen * index
    spread = jnp.zeros((owners, slots), f32)
    for c in range(CAP):
        column = jnp.sum(asked[c], axis=1, keepdims=True)
        spread = spread + jnp.where(lane == lax.rem(own_row, n_c) * CAP + c, column, 0.0)
    want = jnp.sum(spread.reshape(n_z, n_c, slots), axis=1)
    for z in range(n_z):
        want_s[z] = want[z : z + 1]
    pl.semaphore_wait(barrier, n_z + n_c + n_view - 3)

    copies = exchange(n_z, z_peer, sem_z, 0, lambda o: want_s.at[o], lambda s: ask_a.at[my_z])
    ask_a[my_z] = want_s[my_z]
    finish(copies)
    copies = exchange(n_c, c_peer, sem_c, 0, lambda o: ask_a, lambda s: ask_b.at[my_c])
    ask_b[my_c] = ask_a[...]
    finish(copies)
    asks = ask_b[...].reshape(owners, slots)
    params = params_ref[...]
    place = lax.broadcasted_iota(jnp.int32, (owners, g_dev), 1) + 1
    answers = []
    for c in range(CAP):
        column = jnp.sum(jnp.where(lane == my_c * CAP + c, asks, 0.0), axis=1, keepdims=True)
        hot = jnp.where(place == column.astype(jnp.int32), 1.0, 0.0).astype(bf16)
        hot_s[c] = hot
        answers.append(dot(hot, params, ((1,), (1,))))
    par_x[...] = jnp.concatenate(answers, axis=1).astype(bf16).reshape(par_x.shape)

    copies = exchange(n_c, c_peer, sem_c, 1, lambda o: par_x.at[o], lambda s: par_y.at[my_c])
    par_y[my_c] = par_x[my_c]
    finish(copies)
    block = par_y[...].astype(f32)
    for z in range(n_z):
        par_s[z] = block[:, z, :].astype(bf16)
    copies = exchange(n_z, z_peer, sem_z, 1, lambda o: par_s.at[o], lambda s: par_q.at[my_z])
    par_q[my_z] = par_s[my_z]
    finish(copies)
    turned = par_q[...].astype(f32).reshape(owners, CAP * width).T
    rows = jnp.zeros((width, n_tiles * slots), f32)
    for c in range(CAP):
        rows = rows + dot(
            turned[c * width : (c + 1) * width].astype(bf16), pick_s[c], ((1,), (0,))
        )
    for t in range(n_tiles):
        rows_s[:, t, :] = rows[:, t * slots : (t + 1) * slots]

    render_tiles(
        rows_s, ids_ref, pos_ref, cam_ref, cams_ref, target_ref, picture_ref,
        dx_s, dy_s, exp_s, alpha_s, trans_s, color_s,
    )

    grads = jnp.concatenate([rows_s[:, t, :] for t in range(n_tiles)], axis=1)
    parts = pieces(grads)
    sums = []
    for c in range(CAP):
        pick = pick_s[c]
        sums.append(sum(dot(pick, part, ((1,), (1,))) for part in parts))
    grad_s[...] = jnp.concatenate(sums, axis=1).reshape(grad_s.shape)
    copies = exchange(n_z, z_peer, sem_z, 2, lambda o: grad_s.at[o], lambda s: grad_y.at[my_z])
    grad_y[my_z] = grad_s[my_z]
    finish(copies)
    for c in range(n_c):
        grad_x[c] = grad_y[:, c, :]
    copies = exchange(n_c, c_peer, sem_c, 2, lambda o: grad_x.at[o], lambda s: grad_u.at[my_c])
    grad_u[my_c] = grad_x[my_c]
    finish(copies)
    turned = grad_u[...].reshape(owners, CAP * width).T
    total = jnp.zeros((width, g_dev), f32)
    for c in range(CAP):
        for part in pieces(turned[c * width : (c + 1) * width]):
            total = total + dot(part, hot_s[c], ((1,), (0,)))

    chunk = width // n_view
    local[...] = total.reshape(local.shape)
    finish(exchange(n_view, v_peer, sem_v, 0, lambda o: local.at[o], lambda s: arrived.at[s - 1]))
    mine = local[my_view]
    for step in range(1, n_view):
        mine = mine + arrived[step - 1]
    gathered[0] = mine
    finish(exchange(n_view, v_peer, sem_v, 1, lambda o: gathered.at[0], lambda s: gathered.at[s]))
    for step in range(n_view):
        origin = lax.rem(my_view + n_view - step, n_view)
        out_ref[pl.ds(pl.multiple_of(origin * chunk, chunk), chunk)] = gathered[step]


def on_device(params, lists, tile_pos, cam_index, cams, targets):
    owners = lax.axis_size("gauss")
    n_view = lax.axis_size("view")
    n_c = max(2, owners // 16)
    n_z = owners // n_c
    width, g_dev = params.shape
    n_tiles, slots = lists.shape
    half = targets.shape[2] // 2
    line = CAP * width
    chunk = width // n_view
    f32, bf16 = jnp.float32, jnp.bfloat16
    vmem = pl.BlockSpec(memory_space=pltpu.VMEM)
    smem = pl.BlockSpec(memory_space=pltpu.SMEM)
    plane = (slots, 2 * n_tiles, half)
    shapes = [
        ((n_z, 1, slots), f32),
        ((n_z, 1, slots), f32),
        ((n_c, n_z, 1, slots), f32),
        ((n_c, n_z, line), bf16),
        ((n_c, n_z, line), bf16),
        ((n_z, n_c, line), bf16),
        ((n_z, n_c, line), bf16),
        ((width, n_tiles, slots), f32),
        ((n_z, n_c, line), f32),
        ((n_z, n_c, line), f32),
        ((n_c, n_z, line), f32),
        ((n_c, n_z, line), f32),
        ((CAP, owners, g_dev), bf16),
        ((CAP, owners, n_tiles * slots), bf16),
        (plane, f32),
        (plane, f32),
        (plane, f32),
        (plane, f32),
        (plane, f32),
        ((3,) + plane, f32),
        ((n_view, chunk, g_dev), f32),
        ((n_view - 1, chunk, g_dev), f32),
        ((n_view, chunk, g_dev), f32),
    ]
    return pl.pallas_call(
        lambda *refs: step_kernel(n_view, n_z, n_c, *refs),
        out_shape=(
            jax.ShapeDtypeStruct(targets.shape, f32),
            jax.ShapeDtypeStruct((width, g_dev), f32),
        ),
        in_specs=[vmem, vmem, smem, smem, smem, vmem],
        out_specs=(vmem, vmem),
        scratch_shapes=[pltpu.VMEM(shape, dtype) for shape, dtype in shapes]
        + [
            pltpu.SemaphoreType.DMA((3, 2, n_z - 1)),
            pltpu.SemaphoreType.DMA((3, 2, n_c - 1)),
            pltpu.SemaphoreType.DMA((2, 2, n_view - 1)),
        ],
        compiler_params=pltpu.CompilerParams(collective_id=0, has_side_effects=True),
    )(params, lists, tile_pos, cam_index, cams, targets)


def solution(mesh):
    return jax.shard_map(
        on_device,
        mesh=mesh,
        in_specs=(
            P(None, "gauss"),
            P(("gauss", "view"), None),
            P(("gauss", "view")),
            P(("gauss", "view")),
            P(),
            P(None, ("gauss", "view"), None),
        ),
        out_specs=(P(None, ("gauss", "view"), None), P(None, "gauss")),
        check_vma=False,
    )
```

```python
import jax
import jax.numpy as jnp
from jax import lax
from jax.experimental import pallas as pl
from jax.experimental.pallas import tpu as pltpu
from jax.sharding import PartitionSpec as P

WIN = 16


def sh_terms(dir_x, dir_y, dir_z):
    return [
        jnp.ones_like(dir_x),
        dir_x,
        dir_y,
        dir_z,
        dir_x * dir_y,
        dir_y * dir_z,
        dir_x * dir_z,
        dir_x * dir_x - dir_y * dir_y,
        3.0 * dir_z * dir_z - 1.0,
        dir_x * (dir_x * dir_x - 3.0 * dir_y * dir_y),
        dir_x * dir_y * dir_z,
        dir_y * (3.0 * dir_x * dir_x - dir_y * dir_y),
        dir_z * (dir_x * dir_x - dir_y * dir_y),
        dir_x * (5.0 * dir_z * dir_z - 1.0),
        dir_y * (5.0 * dir_z * dir_z - 1.0),
        dir_z * (5.0 * dir_z * dir_z - 3.0),
    ]


def project(row_vals, camcols):
    mean_x, mean_y, mean_z = (row_vals[0], row_vals[1], row_vals[2])
    cam_rot = [camcols[index] for index in range(9)]
    focal = camcols[12]
    cam_x = cam_rot[0] * mean_x + cam_rot[1] * mean_y + cam_rot[2] * mean_z + camcols[9]
    cam_y = cam_rot[3] * mean_x + cam_rot[4] * mean_y + cam_rot[5] * mean_z + camcols[10]
    cam_z = cam_rot[6] * mean_x + cam_rot[7] * mean_y + cam_rot[8] * mean_z + camcols[11]
    inv_z = 1.0 / cam_z
    quaternion = row_vals[6:10]
    q_norm = jnp.sqrt(
        quaternion[0] * quaternion[0]
        + quaternion[1] * quaternion[1]
        + quaternion[2] * quaternion[2]
        + quaternion[3] * quaternion[3]
    )
    unit_w = quaternion[0] / q_norm
    unit_x = quaternion[1] / q_norm
    unit_y = quaternion[2] / q_norm
    unit_z = quaternion[3] / q_norm
    rotation = [
        [
            1.0 - 2.0 * (unit_y * unit_y + unit_z * unit_z),
            2.0 * (unit_x * unit_y - unit_w * unit_z),
            2.0 * (unit_x * unit_z + unit_w * unit_y),
        ],
        [
            2.0 * (unit_x * unit_y + unit_w * unit_z),
            1.0 - 2.0 * (unit_x * unit_x + unit_z * unit_z),
            2.0 * (unit_y * unit_z - unit_w * unit_x),
        ],
        [
            2.0 * (unit_x * unit_z - unit_w * unit_y),
            2.0 * (unit_y * unit_z + unit_w * unit_x),
            1.0 - 2.0 * (unit_x * unit_x + unit_y * unit_y),
        ],
    ]
    mixed = [
        [
            cam_rot[3 * row_i] * rotation[0][col_k]
            + cam_rot[3 * row_i + 1] * rotation[1][col_k]
            + cam_rot[3 * row_i + 2] * rotation[2][col_k]
            for col_k in range(3)
        ]
        for row_i in range(3)
    ]
    jac_scale = focal * inv_z
    proj_u = [
        jac_scale * mixed[0][col_k] - jac_scale * cam_x * inv_z * mixed[2][col_k]
        for col_k in range(3)
    ]
    proj_v = [
        jac_scale * mixed[1][col_k] - jac_scale * cam_y * inv_z * mixed[2][col_k]
        for col_k in range(3)
    ]
    var_diag = [jnp.exp(2.0 * row_vals[axis]) for axis in range(3, 6)]
    cov_a = (
        proj_u[0] * proj_u[0] * var_diag[0]
        + proj_u[1] * proj_u[1] * var_diag[1]
        + proj_u[2] * proj_u[2] * var_diag[2]
        + 0.3
    )
    cov_b = (
        proj_u[0] * proj_v[0] * var_diag[0]
        + proj_u[1] * proj_v[1] * var_diag[1]
        + proj_u[2] * proj_v[2] * var_diag[2]
    )
    cov_c = (
        proj_v[0] * proj_v[0] * var_diag[0]
        + proj_v[1] * proj_v[1] * var_diag[1]
        + proj_v[2] * proj_v[2] * var_diag[2]
        + 0.3
    )
    determinant = cov_a * cov_c - cov_b * cov_b
    opacity = jax.nn.sigmoid(row_vals[10])
    distance = jnp.sqrt(cam_x * cam_x + cam_y * cam_y + cam_z * cam_z)
    terms = sh_terms(cam_x / distance, cam_y / distance, cam_z / distance)
    colors = []
    for chan in range(3):
        shade = 0.5 + sum(
            (row_vals[11 + 16 * chan + basis_b] * terms[basis_b] for basis_b in range(16))
        )
        shade = shade + sum(
            (row_vals[59 + feat_j] * camcols[13 + 3 * feat_j + chan] for feat_j in range(5))
        )
        colors.append(shade)
    centre_u = focal * cam_x * inv_z
    centre_v = focal * cam_y * inv_z
    return [
        centre_u,
            centre_v,
            cov_c / determinant,
            -cov_b / determinant,
            cov_a / determinant,
            opacity,
            colors[0],
            colors[1],
            colors[2],
    ]


def tile_values(scalars, shape):
    tile = lax.broadcasted_iota(jnp.int32, shape, 0) % len(scalars)
    out = jnp.full(shape, scalars[0])
    for index, value in enumerate(scalars[1:], 1):
        out = jnp.where(tile == index, value, out)
    return out


CAP = 4
ATTRS = 9


def render_tiles(
    attr_ref, pos_ref, target_ref, picture_ref,
    dx_s, dy_s, exp_s, alpha_s, trans_s, color_s,
):
    n_tiles, slots = attr_ref.shape[1:]
    half = target_ref.shape[2] // 2
    wide = (2 * n_tiles, half)
    attrs = [attr_ref[row] for row in range(ATTRS)]
    attrs8 = [jnp.concatenate([a, a], axis=0) for a in attrs]

    row_id = lax.broadcasted_iota(jnp.int32, wide, 0)
    lane = lax.broadcasted_iota(jnp.int32, wide, 1)
    pixel = lane + jnp.where(row_id >= n_tiles, half, 0)
    base_x = tile_values([16 * (pos_ref[t] % WIN - WIN // 2) for t in range(n_tiles)], wide)
    base_y = tile_values([16 * (pos_ref[t] // WIN - WIN // 2) for t in range(n_tiles)], wide)
    pixel_x = (base_x + pixel % 16).astype(jnp.float32) + 0.5
    pixel_y = (base_y + pixel // 16).astype(jnp.float32) + 0.5

    def spread(values, slot):
        at = jnp.full(wide, slot, jnp.int32)
        return jnp.take_along_axis(values, at, axis=1, mode="promise_in_bounds")

    unroll = 8

    def forward(step, carry):
        trans, r0, r1, r2 = carry
        for inner in range(unroll):
            slot = step * unroll + inner
            u, v, ca, cb, cc, op, c0, c1, c2 = [spread(a, slot) for a in attrs8]
            dx = pixel_x - u
            dy = pixel_y - v
            power = -0.5 * (ca * dx * dx + 2.0 * cb * dx * dy + cc * dy * dy)
            e = jnp.exp(power)
            alpha = op * e
            dx_s[slot] = dx
            dy_s[slot] = dy
            exp_s[slot] = e
            alpha_s[slot] = alpha
            trans_s[slot] = trans
            color_s[0, slot] = c0
            color_s[1, slot] = c1
            color_s[2, slot] = c2
            w = alpha * trans
            r0, r1, r2 = r0 + c0 * w, r1 + c1 * w, r2 + c2 * w
            trans = trans * (1.0 - alpha)
        return trans, r0, r1, r2

    zero = jnp.zeros(wide, jnp.float32)
    _, r0, r1, r2 = lax.fori_loop(
        0, slots // unroll, forward, (jnp.ones(wide, jnp.float32), zero, zero, zero)
    )
    res = []
    for chan, pic in enumerate((r0, r1, r2)):
        picture_ref[chan, :, :half] = pic[:n_tiles]
        picture_ref[chan, :, half:] = pic[n_tiles:]
        want = target_ref[chan]
        res.append(pic - jnp.concatenate([want[:, :half], want[:, half:]], axis=0))

    def backward(step, carry):
        behind, accs = carry
        accs = list(accs)
        for inner in range(unroll):
            slot = slots - 1 - (step * unroll + inner)
            dx, dy, e, alpha, trans = dx_s[slot], dy_s[slot], exp_s[slot], alpha_s[slot], trans_s[slot]
            q = color_s[0, slot] * res[0] + color_s[1, slot] * res[1] + color_s[2, slot] * res[2]
            w = alpha * trans
            diff = q - behind
            gain = trans * diff * e
            behind = behind + alpha * diff
            gx = gain * dx
            gy = gain * dy
            terms = [gain, gx, gy, gx * dx, gx * dy, gy * dy, w * res[0], w * res[1], w * res[2]]
            here = lane == slot
            for index, term in enumerate(terms):
                total = jnp.sum(term, axis=1, keepdims=True)
                accs[index] = jnp.where(here, total, accs[index])
        return behind, tuple(accs)

    _, accs = lax.fori_loop(0, slots // unroll, backward, (zero, (zero,) * 9))
    g0, gx, gy, gxx, gxy, gyy, k0, k1, k2 = [a[:n_tiles] + a[n_tiles:] for a in accs]
    op = attrs[5]
    ca, cb, cc = attrs[2:5]
    cot = [
        op * (ca * gx + cb * gy),
        op * (cb * gx + cc * gy),
        -0.5 * (op * gxx),
        -(op * gxy),
        -0.5 * (op * gyy),
        g0,
        k0,
        k1,
        k2,
    ]
    for row, value in enumerate(cot):
        attr_ref[row] = value


def pieces(values):
    out = []
    for _ in range(3):
        out.append(values.astype(jnp.bfloat16))
        values = values - out[-1].astype(jnp.float32)
    return jnp.concatenate(out, axis=0)


def joined(values):
    third = values.shape[0] // 3
    return values[:third] + values[third : 2 * third] + values[2 * third :]


def dot(a, b, dims):
    return lax.dot_general(a, b, (dims, ((), ())), preferred_element_type=jnp.float32)


def step_kernel(
    n_view, n_z, n_c,
    params_ref, ids_ref, pos_ref, cam_ref, cams_ref, target_ref,
    picture_ref, out_ref,
    want_s, ask_a, ask_b, par_t, par_x, par_y, par_s, par_q, own_s, cam_s, all_s, all_cam_s,
    attr_s, grad_s, grad_y, grad_x, grad_u, cot_s, hot_s, pick_s,
    dx_s, dy_s, exp_s, alpha_s, trans_s, color_s,
    sem_z, sem_c, sem_g,
):
    owners = n_z * n_c
    width, g_dev = params_ref.shape
    n_tiles, slots = ids_ref.shape
    f32, bf16 = jnp.float32, jnp.bfloat16
    me = lax.axis_index("gauss")
    my_view = lax.axis_index("view")
    my_z, my_c = me // n_c, lax.rem(me, n_c)

    def z_peer(step):
        other = lax.rem(my_z + step, n_z)
        return other, {"gauss": other * n_c + my_c}

    def cv_peer(step):
        other = lax.rem(my_c + step % n_c, n_c)
        return other, {
            "gauss": my_z * n_c + other,
            "view": lax.rem(my_view + step // n_c, n_view),
        }

    barrier = pltpu.get_barrier_semaphore()
    for count, peer in ((n_z, z_peer), (n_c * n_view, cv_peer)):
        for step in range(1, count):
            pl.semaphore_signal(
                barrier, inc=1, device_id=peer(step)[1], device_id_type=pl.DeviceIdType.MESH
            )

    def exchange(count, peer, sems, source, target):
        copies = []
        for step in range(1, count):
            other, device = peer(step)
            copy = pltpu.make_async_remote_copy(
                src_ref=source(other),
                dst_ref=target,
                send_sem=sems.at[0, step - 1],
                recv_sem=sems.at[1, step - 1],
                device_id=device,
                device_id_type=pl.DeviceIdType.MESH,
            )
            copy.start()
            copies.append(copy)
        return copies

    def finish(copies):
        for copy in copies:
            copy.wait()

    bits = g_dev.bit_length() - 1
    base = 2 * g_dev
    own_row = lax.broadcasted_iota(jnp.int32, (owners, slots), 0)
    lane = lax.broadcasted_iota(jnp.int32, (owners, slots), 1)
    before = (
        lax.broadcasted_iota(jnp.int32, (slots, slots), 0)
        < lax.broadcasted_iota(jnp.int32, (slots, slots), 1)
    )
    before = jnp.where(before, 1.0, 0.0).astype(bf16)
    seen = jnp.zeros((owners, 1), f32)
    asked = [jnp.zeros((owners, slots), f32) for _ in range(CAP)]
    for t in range(n_tiles):
        ids = ids_ref[t : t + 1, :]
        owner = lax.shift_right_arithmetic(ids, bits)
        code = (lax.bitwise_and(ids, g_dev - 1) + (1 + base * cam_ref[t])).astype(f32)
        named = own_row == owner
        named_f = jnp.where(named, 1.0, 0.0)
        rank = dot(named_f.astype(bf16), before, ((1,), (0,))) + seen
        seen = seen + jnp.sum(named_f, axis=1, keepdims=True)
        for c in range(CAP):
            chosen = jnp.where(rank == float(c), named_f, 0.0)
            pick_s[c * owners : (c + 1) * owners, t * slots : (t + 1) * slots] = chosen.astype(bf16)
            asked[c] = asked[c] + chosen * code
    spread = jnp.zeros((owners, slots), f32)
    for c in range(CAP):
        column = jnp.sum(asked[c], axis=1, keepdims=True)
        spread = spread + jnp.where(lane == lax.rem(own_row, n_c) * CAP + c, column, 0.0)
    want = jnp.sum(spread.reshape(n_z, n_c, slots), axis=1)
    for z in range(n_z):
        want_s[z] = want[z : z + 1]
    par_t[...] = jnp.zeros(par_t.shape, f32)
    pl.semaphore_wait(barrier, n_z + n_c * n_view - 2)

    copies = exchange(n_z, z_peer, sem_z.at[0], lambda o: want_s.at[o], ask_a.at[my_z])
    ask_a[my_z] = want_s[my_z]
    finish(copies)
    asking = exchange(
        n_c * n_view, cv_peer, sem_g.at[0], lambda o: ask_a, ask_b.at[my_view, my_c]
    )
    ask_b[my_view, my_c] = ask_a[...]
    finish(asking[: n_c - 1])

    params = params_ref[...]
    cams3 = pieces(cams_ref[...].T)
    n_src = n_z * n_c
    place = lax.broadcasted_iota(jnp.int32, (g_dev, n_src), 0) + 1
    camera = lax.broadcasted_iota(jnp.int32, (cams_ref.shape[0], n_src), 0)
    row8 = lax.broadcasted_iota(jnp.int32, (8, slots), 0)
    lane8 = lax.broadcasted_iota(jnp.int32, (8, slots), 1)
    mine8 = jnp.where(lane8 == my_c * CAP + row8, 1.0, 0.0).astype(bf16)

    def look_up(asks, rows_ref, cams_out, hot_ref, first):
        asks = asks.reshape(n_src, slots)
        codes = jnp.zeros((8, n_src), f32)
        rest = asks
        for _ in range(2):
            part = rest.astype(bf16)
            rest = rest - part.astype(f32)
            codes = codes + dot(mine8, part, ((1,), (1,)))
        codes = codes.astype(jnp.int32)
        index = lax.bitwise_and(codes, base - 1)
        seen_by = lax.shift_right_logical(codes, bits + 1)
        for c in range(CAP):
            hot = jnp.where(place == index[c : c + 1], 1.0, 0.0).astype(bf16)
            if hot_ref is not None:
                hot_ref[:, c * n_src : (c + 1) * n_src] = hot
            rows_ref[:, first + c, :] = dot(params, hot, ((1,), (0,)))
            chosen = jnp.where(camera == seen_by[c : c + 1], 1.0, 0.0).astype(bf16)
            cams_out[:, first + c, :] = joined(dot(cams3, chosen, ((1,), (0,))))
        return index[:CAP] > 0

    def safe(rows_ref, cams_in, live):
        row_vals = [rows_ref[row] for row in range(width)]
        row_vals[6] = jnp.where(live, row_vals[6], 1.0)
        camcols = [cams_in[row] for row in range(cams_ref.shape[1])]
        camcols[11] = jnp.where(live, camcols[11], 4.0)
        return row_vals, camcols

    live = look_up(ask_b[my_view], own_s, cam_s, None, 0)
    row_vals, camcols = safe(own_s, cam_s, live)
    for index, value in enumerate(project(row_vals, camcols)):
        par_t[:CAP, index, :] = value
    par_x[...] = par_t[...].reshape(8 * 16, n_src).T.reshape(par_x.shape)

    copies = exchange(n_c, cv_peer, sem_c, lambda o: par_x.at[o], par_y.at[my_c])
    par_y[my_c] = par_x[my_c]
    finish(copies)
    for z in range(n_z):
        par_s[z] = par_y[:, z, :]
    copies = exchange(n_z, z_peer, sem_z.at[1], lambda o: par_s.at[o], par_q.at[my_z])
    par_q[my_z] = par_s[my_z]

    finish(asking[n_c - 1 :])
    lives = [
        look_up(ask_b[v], all_s, all_cam_s, hot_s.at[v], v * CAP) for v in range(n_view)
    ]
    all_live = jnp.concatenate([jnp.where(a, 1.0, 0.0) for a in lives], axis=0) > 0.5
    row_vals, camcols = safe(all_s, all_cam_s, all_live)
    finish(copies)

    turned = par_q[...].reshape(owners, 128).T
    left = jnp.concatenate([pieces(turned[c * 16 : (c + 1) * 16]) for c in range(CAP)], axis=1)
    found = joined(dot(left, pick_s[...], ((1,), (0,))))
    for t in range(n_tiles):
        attr_s[:, t, :] = found[:, t * slots : (t + 1) * slots]

    render_tiles(
        attr_s, pos_ref, target_ref, picture_ref,
        dx_s, dy_s, exp_s, alpha_s, trans_s, color_s,
    )

    grads = jnp.concatenate([attr_s[:, t, :] for t in range(n_tiles)], axis=1)
    sums = joined(dot(pieces(grads), pick_s[...], ((1,), (1,))))
    sums = jnp.concatenate(
        [sums[:, c * owners : (c + 1) * owners] for c in range(CAP)]
        + [jnp.zeros((128 - 16 * CAP, owners), f32)],
        axis=0,
    )
    grad_s[...] = sums.T.reshape(grad_s.shape)
    copies = exchange(n_z, z_peer, sem_z.at[2], lambda o: grad_s.at[o], grad_y.at[my_z])
    grad_y[my_z] = grad_s[my_z]
    finish(copies)
    for c in range(n_c):
        grad_x[c] = grad_y[:, c, :]
    copies = exchange(
        n_c * n_view, cv_peer, sem_g.at[1], lambda o: grad_x.at[o], grad_u.at[my_view, my_c]
    )
    grad_u[my_view, my_c] = grad_x[my_c]
    _, pullback = jax.vjp(lambda vals: project(vals, camcols), row_vals)
    finish(copies)
    for v in range(n_view):
        turned = grad_u[v].reshape(n_src, 128).T
        for c in range(CAP):
            cot_s[v * CAP + c] = turned[c * 16 : (c + 1) * 16]
    (grads,) = pullback([cot_s[:, index, :] for index in range(ATTRS)])
    for row, value in enumerate(grads):
        all_s[row] = value
    total = jnp.zeros((3 * width, g_dev), f32)
    for v in range(n_view):
        line = jnp.concatenate([all_s[:, v * CAP + c, :] for c in range(CAP)], axis=1)
        total = total + dot(pieces(line), hot_s[v], ((1,), (1,)))
    out_ref[...] = joined(total)


def on_device(params, lists, tile_pos, cam_index, cams, targets):
    owners = lax.axis_size("gauss")
    n_view = lax.axis_size("view")
    n_c = max(2, owners // 16)
    n_z = owners // n_c
    width, g_dev = params.shape
    n_tiles, slots = lists.shape
    half = targets.shape[2] // 2
    rows_c = cams.shape[0]
    f32, bf16 = jnp.float32, jnp.bfloat16
    vmem = pl.BlockSpec(memory_space=pltpu.VMEM)
    smem = pl.BlockSpec(memory_space=pltpu.SMEM)
    plane = (slots, 2 * n_tiles, half)
    shapes = [
        ((n_z, 1, slots), f32),
        ((n_z, 1, slots), f32),
        ((n_view, n_c, n_z, 1, slots), f32),
        ((8, 16, owners), f32),
        ((n_c, n_z, 128), f32),
        ((n_c, n_z, 128), f32),
        ((n_z, n_c, 128), f32),
        ((n_z, n_c, 128), f32),
        ((width, CAP, owners), f32),
        ((rows_c, CAP, owners), f32),
        ((width, n_view * CAP, owners), f32),
        ((rows_c, n_view * CAP, owners), f32),
        ((16, n_tiles, slots), f32),
        ((n_z, n_c, 128), f32),
        ((n_z, n_c, 128), f32),
        ((n_c, n_z, 128), f32),
        ((n_view, n_c, n_z, 128), f32),
        ((n_view * CAP, 16, owners), f32),
        ((n_view, g_dev, CAP * owners), bf16),
        ((CAP * owners, n_tiles * slots), bf16),
        (plane, f32),
        (plane, f32),
        (plane, f32),
        (plane, f32),
        (plane, f32),
        ((3,) + plane, f32),
    ]
    return pl.pallas_call(
        lambda *refs: step_kernel(n_view, n_z, n_c, *refs),
        out_shape=(
            jax.ShapeDtypeStruct(targets.shape, f32),
            jax.ShapeDtypeStruct((width, g_dev), f32),
        ),
        in_specs=[vmem, vmem, smem, smem, vmem, vmem],
        out_specs=(vmem, vmem),
        scratch_shapes=[pltpu.VMEM(shape, dtype) for shape, dtype in shapes]
        + [
            pltpu.SemaphoreType.DMA((3, 2, n_z - 1)),
            pltpu.SemaphoreType.DMA((2, n_c - 1)),
            pltpu.SemaphoreType.DMA((2, 2, n_c * n_view - 1)),
        ],
        compiler_params=pltpu.CompilerParams(collective_id=0, has_side_effects=True),
    )(params, lists, tile_pos, cam_index, cams.T, targets)


def solution(mesh):
    return jax.shard_map(
        on_device,
        mesh=mesh,
        in_specs=(
            P(None, "gauss"),
            P(("gauss", "view"), None),
            P(("gauss", "view")),
            P(("gauss", "view")),
            P(),
            P(None, ("gauss", "view"), None),
        ),
        out_specs=(P(None, ("gauss", "view"), None), P(None, "gauss")),
        check_vma=False,
    )
```

```python
import jax
import jax.numpy as jnp
from jax import lax
from jax.experimental import pallas as pl
from jax.experimental.pallas import tpu as pltpu
from jax.sharding import PartitionSpec as P

WIN = 16


def sh_terms(dir_x, dir_y, dir_z):
    return [
        jnp.ones_like(dir_x),
        dir_x,
        dir_y,
        dir_z,
        dir_x * dir_y,
        dir_y * dir_z,
        dir_x * dir_z,
        dir_x * dir_x - dir_y * dir_y,
        3.0 * dir_z * dir_z - 1.0,
        dir_x * (dir_x * dir_x - 3.0 * dir_y * dir_y),
        dir_x * dir_y * dir_z,
        dir_y * (3.0 * dir_x * dir_x - dir_y * dir_y),
        dir_z * (dir_x * dir_x - dir_y * dir_y),
        dir_x * (5.0 * dir_z * dir_z - 1.0),
        dir_y * (5.0 * dir_z * dir_z - 1.0),
        dir_z * (5.0 * dir_z * dir_z - 3.0),
    ]


def project(row_vals, camcols):
    mean_x, mean_y, mean_z = (row_vals[0], row_vals[1], row_vals[2])
    cam_rot = [camcols[index] for index in range(9)]
    focal = camcols[12]
    cam_x = cam_rot[0] * mean_x + cam_rot[1] * mean_y + cam_rot[2] * mean_z + camcols[9]
    cam_y = cam_rot[3] * mean_x + cam_rot[4] * mean_y + cam_rot[5] * mean_z + camcols[10]
    cam_z = cam_rot[6] * mean_x + cam_rot[7] * mean_y + cam_rot[8] * mean_z + camcols[11]
    inv_z = 1.0 / cam_z
    quaternion = row_vals[6:10]
    q_norm = jnp.sqrt(
        quaternion[0] * quaternion[0]
        + quaternion[1] * quaternion[1]
        + quaternion[2] * quaternion[2]
        + quaternion[3] * quaternion[3]
    )
    unit_w = quaternion[0] / q_norm
    unit_x = quaternion[1] / q_norm
    unit_y = quaternion[2] / q_norm
    unit_z = quaternion[3] / q_norm
    rotation = [
        [
            1.0 - 2.0 * (unit_y * unit_y + unit_z * unit_z),
            2.0 * (unit_x * unit_y - unit_w * unit_z),
            2.0 * (unit_x * unit_z + unit_w * unit_y),
        ],
        [
            2.0 * (unit_x * unit_y + unit_w * unit_z),
            1.0 - 2.0 * (unit_x * unit_x + unit_z * unit_z),
            2.0 * (unit_y * unit_z - unit_w * unit_x),
        ],
        [
            2.0 * (unit_x * unit_z - unit_w * unit_y),
            2.0 * (unit_y * unit_z + unit_w * unit_x),
            1.0 - 2.0 * (unit_x * unit_x + unit_y * unit_y),
        ],
    ]
    mixed = [
        [
            cam_rot[3 * row_i] * rotation[0][col_k]
            + cam_rot[3 * row_i + 1] * rotation[1][col_k]
            + cam_rot[3 * row_i + 2] * rotation[2][col_k]
            for col_k in range(3)
        ]
        for row_i in range(3)
    ]
    jac_scale = focal * inv_z
    proj_u = [
        jac_scale * mixed[0][col_k] - jac_scale * cam_x * inv_z * mixed[2][col_k]
        for col_k in range(3)
    ]
    proj_v = [
        jac_scale * mixed[1][col_k] - jac_scale * cam_y * inv_z * mixed[2][col_k]
        for col_k in range(3)
    ]
    var_diag = [jnp.exp(2.0 * row_vals[axis]) for axis in range(3, 6)]
    cov_a = (
        proj_u[0] * proj_u[0] * var_diag[0]
        + proj_u[1] * proj_u[1] * var_diag[1]
        + proj_u[2] * proj_u[2] * var_diag[2]
        + 0.3
    )
    cov_b = (
        proj_u[0] * proj_v[0] * var_diag[0]
        + proj_u[1] * proj_v[1] * var_diag[1]
        + proj_u[2] * proj_v[2] * var_diag[2]
    )
    cov_c = (
        proj_v[0] * proj_v[0] * var_diag[0]
        + proj_v[1] * proj_v[1] * var_diag[1]
        + proj_v[2] * proj_v[2] * var_diag[2]
        + 0.3
    )
    determinant = cov_a * cov_c - cov_b * cov_b
    opacity = jax.nn.sigmoid(row_vals[10])
    distance = jnp.sqrt(cam_x * cam_x + cam_y * cam_y + cam_z * cam_z)
    terms = sh_terms(cam_x / distance, cam_y / distance, cam_z / distance)
    colors = []
    for chan in range(3):
        shade = 0.5 + sum(
            (row_vals[11 + 16 * chan + basis_b] * terms[basis_b] for basis_b in range(16))
        )
        shade = shade + sum(
            (row_vals[59 + feat_j] * camcols[13 + 3 * feat_j + chan] for feat_j in range(5))
        )
        colors.append(shade)
    centre_u = focal * cam_x * inv_z
    centre_v = focal * cam_y * inv_z
    return [
        centre_u,
            centre_v,
            cov_c / determinant,
            -cov_b / determinant,
            cov_a / determinant,
            opacity,
            colors[0],
            colors[1],
            colors[2],
    ]


def tile_values(scalars, shape):
    tile = lax.broadcasted_iota(jnp.int32, shape, 0) % len(scalars)
    out = jnp.full(shape, scalars[0])
    for index, value in enumerate(scalars[1:], 1):
        out = jnp.where(tile == index, value, out)
    return out


CAP = 4
ATTRS = 9


def render_tiles(
    attr_ref, pos_ref, target_ref, picture_ref,
    dx_s, dy_s, exp_s, alpha_s, trans_s, color_s,
):
    n_tiles, slots = attr_ref.shape[1:]
    half = target_ref.shape[2] // 2
    wide = (2 * n_tiles, half)
    attrs = [attr_ref[row] for row in range(ATTRS)]
    attrs8 = [jnp.concatenate([a, a], axis=0) for a in attrs]

    row_id = lax.broadcasted_iota(jnp.int32, wide, 0)
    lane = lax.broadcasted_iota(jnp.int32, wide, 1)
    pixel = lane + jnp.where(row_id >= n_tiles, half, 0)
    base_x = tile_values([16 * (pos_ref[t] % WIN - WIN // 2) for t in range(n_tiles)], wide)
    base_y = tile_values([16 * (pos_ref[t] // WIN - WIN // 2) for t in range(n_tiles)], wide)
    pixel_x = (base_x + pixel % 16).astype(jnp.float32) + 0.5
    pixel_y = (base_y + pixel // 16).astype(jnp.float32) + 0.5

    def spread(values, slot):
        at = jnp.full(wide, slot, jnp.int32)
        return jnp.take_along_axis(values, at, axis=1, mode="promise_in_bounds")

    unroll = 8

    def forward(step, carry):
        trans, r0, r1, r2 = carry
        for inner in range(unroll):
            slot = step * unroll + inner
            u, v, ca, cb, cc, op, c0, c1, c2 = [spread(a, slot) for a in attrs8]
            dx = pixel_x - u
            dy = pixel_y - v
            power = -0.5 * (ca * dx * dx + 2.0 * cb * dx * dy + cc * dy * dy)
            e = jnp.exp(power)
            alpha = op * e
            dx_s[slot] = dx
            dy_s[slot] = dy
            exp_s[slot] = e
            alpha_s[slot] = alpha
            trans_s[slot] = trans
            color_s[0, slot] = c0
            color_s[1, slot] = c1
            color_s[2, slot] = c2
            w = alpha * trans
            r0, r1, r2 = r0 + c0 * w, r1 + c1 * w, r2 + c2 * w
            trans = trans * (1.0 - alpha)
        return trans, r0, r1, r2

    zero = jnp.zeros(wide, jnp.float32)
    _, r0, r1, r2 = lax.fori_loop(
        0, slots // unroll, forward, (jnp.ones(wide, jnp.float32), zero, zero, zero)
    )
    res = []
    for chan, pic in enumerate((r0, r1, r2)):
        picture_ref[chan, :, :half] = pic[:n_tiles]
        picture_ref[chan, :, half:] = pic[n_tiles:]
        want = target_ref[chan]
        res.append(pic - jnp.concatenate([want[:, :half], want[:, half:]], axis=0))

    def backward(step, carry):
        behind, accs = carry
        accs = list(accs)
        for inner in range(unroll):
            slot = slots - 1 - (step * unroll + inner)
            dx, dy, e, alpha, trans = dx_s[slot], dy_s[slot], exp_s[slot], alpha_s[slot], trans_s[slot]
            q = color_s[0, slot] * res[0] + color_s[1, slot] * res[1] + color_s[2, slot] * res[2]
            w = alpha * trans
            diff = q - behind
            gain = trans * diff * e
            behind = behind + alpha * diff
            gx = gain * dx
            gy = gain * dy
            terms = [gain, gx, gy, gx * dx, gx * dy, gy * dy, w * res[0], w * res[1], w * res[2]]
            here = lane == slot
            for index, term in enumerate(terms):
                total = jnp.sum(term, axis=1, keepdims=True)
                accs[index] = jnp.where(here, total, accs[index])
        return behind, tuple(accs)

    _, accs = lax.fori_loop(0, slots // unroll, backward, (zero, (zero,) * 9))
    g0, gx, gy, gxx, gxy, gyy, k0, k1, k2 = [a[:n_tiles] + a[n_tiles:] for a in accs]
    op = attrs[5]
    ca, cb, cc = attrs[2:5]
    cot = [
        op * (ca * gx + cb * gy),
        op * (cb * gx + cc * gy),
        -0.5 * (op * gxx),
        -(op * gxy),
        -0.5 * (op * gyy),
        g0,
        k0,
        k1,
        k2,
    ]
    for row, value in enumerate(cot):
        attr_ref[row] = value


def pieces(values):
    out = []
    for _ in range(3):
        out.append(values.astype(jnp.bfloat16))
        values = values - out[-1].astype(jnp.float32)
    return jnp.concatenate(out, axis=0)


def two_pieces(values):
    high = values.astype(jnp.bfloat16)
    return high, (values - high.astype(jnp.float32)).astype(jnp.bfloat16)


def swapped(values):
    return pltpu.roll(values, 64, axis=1)


def folded(values):
    count = values.shape[0] // 2
    return values[:count] + swapped(values[count:])


def unfolded(values):
    return jnp.concatenate([values, swapped(values)], axis=0)


def joined(values):
    third = values.shape[0] // 3
    return values[:third] + values[third : 2 * third] + values[2 * third :]


def dot(a, b, dims):
    return lax.dot_general(a, b, (dims, ((), ())), preferred_element_type=jnp.float32)


def step_kernel(
    n_view, n_z, n_c,
    params_hbm, ids_hbm, pos_hbm, cam_hbm, cams_hbm, target_hbm,
    picture_ref, out_ref,
    params_ref, ids_ref, pos_ref, cam_ref, cams_ref, target_ref, sem_in,
    want_s, ask_a, ask_p, ask_b, par_t, par_x, par_y, par_s, par_q, own_s, cam_s, all_s, all_cam_s,
    attr_s, grad_s, grad_y, grad_x, grad_u, cot_s, hot_s, pick_s,
    dx_s, dy_s, exp_s, alpha_s, trans_s, color_s,
    sem_z, sem_c, sem_g,
):
    owners = n_z * n_c
    width, g_dev = params_ref.shape
    n_tiles, slots = ids_ref.shape
    f32, bf16 = jnp.float32, jnp.bfloat16
    me = lax.axis_index("gauss")
    my_view = lax.axis_index("view")
    my_z, my_c = me // n_c, lax.rem(me, n_c)

    def z_peer(step):
        other = lax.rem(my_z + step, n_z)
        return other, {"gauss": other * n_c + my_c}

    def cv_peer(step):
        other = lax.rem(my_c + step % n_c, n_c)
        return other, {
            "gauss": my_z * n_c + other,
            "view": lax.rem(my_view + step // n_c, n_view),
        }

    barrier = pltpu.get_barrier_semaphore()
    for count, peer in ((n_z, z_peer), (n_c * n_view, cv_peer)):
        for step in range(1, count):
            pl.semaphore_signal(
                barrier, inc=1, device_id=peer(step)[1], device_id_type=pl.DeviceIdType.MESH
            )

    loads = [
        pltpu.make_async_copy(source, target, sem_in.at[index])
        for index, (source, target) in enumerate(
            (
                (ids_hbm, ids_ref),
                (cam_hbm, cam_ref),
                (params_hbm, params_ref),
                (cams_hbm, cams_ref),
                (pos_hbm, pos_ref),
                (target_hbm, target_ref),
            )
        )
    ]
    for load in loads:
        load.start()

    def exchange(count, peer, sems, source, target):
        copies = []
        for step in range(1, count):
            other, device = peer(step)
            copy = pltpu.make_async_remote_copy(
                src_ref=source(other),
                dst_ref=target,
                send_sem=sems.at[0, step - 1],
                recv_sem=sems.at[1, step - 1],
                device_id=device,
                device_id_type=pl.DeviceIdType.MESH,
            )
            copy.start()
            copies.append(copy)
        return copies

    def finish(copies):
        for copy in copies:
            copy.wait()

    bits = g_dev.bit_length() - 1
    base = 2 * g_dev
    half_c, half_z, n_q = n_c // 2, n_z // 2, n_z // 4
    row = lax.broadcasted_iota(jnp.int32, (owners, slots), 0)
    row_z = lax.rem(row // half_c, n_z)
    row_c = row // (n_z * half_c) * half_c + lax.rem(row, half_c)
    own_row = row_z * n_c + row_c
    lane = lax.broadcasted_iota(jnp.int32, (owners, slots), 1)
    before = (
        lax.broadcasted_iota(jnp.int32, (slots, slots), 0)
        < lax.broadcasted_iota(jnp.int32, (slots, slots), 1)
    )
    before = jnp.where(before, 1.0, 0.0).astype(bf16)
    seen = jnp.zeros((owners, 1), f32)
    loads[0].wait()
    loads[1].wait()
    asked = [jnp.zeros((owners, slots), f32) for _ in range(CAP)]
    for t in range(n_tiles):
        ids = ids_ref[t : t + 1, :]
        owner = lax.shift_right_arithmetic(ids, bits)
        code = (lax.bitwise_and(ids, g_dev - 1) + (1 + base * cam_ref[t])).astype(f32)
        named = own_row == owner
        named_f = jnp.where(named, 1.0, 0.0)
        rank = dot(named_f.astype(bf16), before, ((1,), (0,))) + seen
        seen = seen + jnp.sum(named_f, axis=1, keepdims=True)
        for c in range(CAP):
            chosen = jnp.where(rank == float(c), named_f, 0.0)
            pick_s[c * owners : (c + 1) * owners, t * slots : (t + 1) * slots] = chosen.astype(bf16)
            asked[c] = asked[c] + chosen * code
    spread = jnp.zeros((owners, slots), f32)
    for c in range(CAP):
        column = jnp.sum(asked[c], axis=1, keepdims=True)
        spread = spread + jnp.where(
            lane == my_z // n_q * 32 + row_c * CAP + c, column, 0.0
        )
    spread = spread[: owners // 2] + spread[owners // 2 :]
    same = lax.broadcasted_iota(jnp.int32, (n_z, owners // 2), 0) == (
        lax.broadcasted_iota(jnp.int32, (n_z, owners // 2), 1) // half_c
    )
    same = jnp.where(same, 1.0, 0.0).astype(bf16)
    want = sum(dot(same, part, ((1,), (0,))) for part in two_pieces(spread))
    for z in range(n_z):
        want_s[z] = want[z : z + 1]
    par_t[...] = jnp.zeros(par_t.shape, f32)
    pl.semaphore_wait(barrier, n_z + n_c * n_view - 2)

    copies = exchange(n_z, z_peer, sem_z.at[0], lambda o: want_s.at[o], ask_a.at[my_z])
    ask_a[my_z] = want_s[my_z]
    finish(copies)
    asked = ask_a[...].reshape(n_z, slots)
    packed = asked[:n_q]
    for part in range(1, 4):
        packed = packed + asked[part * n_q : (part + 1) * n_q]
    ask_p[...] = packed
    asking = exchange(
        n_c * n_view, cv_peer, sem_g.at[0], lambda o: ask_p, ask_b.at[my_view, my_c]
    )
    ask_b[my_view, my_c] = packed
    finish(asking[: n_c - 1])

    loads[2].wait()
    loads[3].wait()
    params = params_ref[...]
    cams3 = pieces(cams_ref[...].T)
    n_src = n_z * n_c
    place = lax.broadcasted_iota(jnp.int32, (g_dev, n_src), 0) + 1
    camera = lax.broadcasted_iota(jnp.int32, (cams_ref.shape[0], n_src), 0)
    row32 = lax.broadcasted_iota(jnp.int32, (32, slots), 0)
    lane32 = lax.broadcasted_iota(jnp.int32, (32, slots), 1)
    mine32 = lane32 == row32 // 8 * 32 + my_c * CAP + lax.rem(row32, 8)
    mine32 = jnp.where(mine32, 1.0, 0.0).astype(bf16)
    line_no = lax.broadcasted_iota(jnp.int32, (n_c * n_q, n_src), 0)
    src = lax.broadcasted_iota(jnp.int32, (n_c * n_q, n_src), 1)
    src_z = src // (n_c * half_z) * half_z + lax.rem(src, half_z)
    src_line = lax.rem(src // half_z, n_c) * n_q + lax.rem(src_z, n_q)
    orders = [
        jnp.where((line_no == src_line) & (src_z // n_q == part), 1.0, 0.0).astype(bf16)
        for part in range(4)
    ]

    def look_up(view, rows_ref, cams_out, hot_ref, first):
        lines = jnp.concatenate([ask_b[view, c] for c in range(n_c)], axis=0)
        found = sum(dot(mine32, part, ((1,), (1,))) for part in two_pieces(lines))
        codes = jnp.zeros((8, n_src), f32)
        for index, order in enumerate(orders):
            for part in two_pieces(found[index * 8 : (index + 1) * 8]):
                codes = codes + dot(part, order, ((1,), (0,)))
        codes = codes.astype(jnp.int32)
        index = lax.bitwise_and(codes, base - 1)
        seen_by = lax.shift_right_logical(codes, bits + 1)
        for c in range(CAP):
            hot = jnp.where(place == index[c : c + 1], 1.0, 0.0).astype(bf16)
            if hot_ref is not None:
                hot_ref[:, c * n_src : (c + 1) * n_src] = hot
            rows_ref[:, first + c, :] = dot(params, hot, ((1,), (0,)))
            chosen = jnp.where(camera == seen_by[c : c + 1], 1.0, 0.0).astype(bf16)
            cams_out[:, first + c, :] = joined(dot(cams3, chosen, ((1,), (0,))))
        return index[:CAP] > 0

    def safe(rows_ref, cams_in, live):
        row_vals = [rows_ref[row] for row in range(width)]
        row_vals[6] = jnp.where(live, row_vals[6], 1.0)
        camcols = [cams_in[row] for row in range(cams_ref.shape[1])]
        camcols[11] = jnp.where(live, camcols[11], 4.0)
        return row_vals, camcols

    live = look_up(my_view, own_s, cam_s, None, 0)
    row_vals, camcols = safe(own_s, cam_s, live)
    for index, value in enumerate(project(row_vals, camcols)):
        par_t[:CAP, index, :] = value
    par_x[...] = folded(par_t[...].reshape(8 * 16, n_src).T).reshape(par_x.shape)

    copies = exchange(n_c, cv_peer, sem_c, lambda o: par_x.at[o], par_y.at[my_c])
    par_y[my_c] = par_x[my_c]
    finish(copies)
    low_c = lax.broadcasted_iota(jnp.int32, (half_c, 128), 1) < 64
    for z in range(half_z):
        lines = par_y[:, z, :]
        other = swapped(lines)
        par_s[z] = jnp.where(low_c, lines[:half_c], other[half_c:])
        par_s[half_z + z] = jnp.where(low_c, other[:half_c], lines[half_c:])
    copies = exchange(n_z, z_peer, sem_z.at[1], lambda o: par_s.at[o], par_q.at[my_z])
    par_q[my_z] = par_s[my_z]

    finish(asking[n_c - 1 :])
    lives = [
        look_up(v, all_s, all_cam_s, hot_s.at[v], v * CAP) for v in range(n_view)
    ]
    all_live = jnp.concatenate([jnp.where(a, 1.0, 0.0) for a in lives], axis=0) > 0.5
    row_vals, camcols = safe(all_s, all_cam_s, all_live)
    finish(copies)

    turned = unfolded(par_q[...].reshape(owners // 2, 128)).T
    left = jnp.concatenate([pieces(turned[c * 16 : (c + 1) * 16]) for c in range(CAP)], axis=1)
    found = joined(dot(left, pick_s[...], ((1,), (0,))))
    for t in range(n_tiles):
        attr_s[:, t, :] = found[:, t * slots : (t + 1) * slots]

    loads[4].wait()
    loads[5].wait()
    render_tiles(
        attr_s, pos_ref, target_ref, picture_ref,
        dx_s, dy_s, exp_s, alpha_s, trans_s, color_s,
    )

    grads = jnp.concatenate([attr_s[:, t, :] for t in range(n_tiles)], axis=1)
    sums = joined(dot(pieces(grads), pick_s[...], ((1,), (1,))))
    sums = jnp.concatenate(
        [sums[:, c * owners : (c + 1) * owners] for c in range(CAP)]
        + [jnp.zeros((128 - 16 * CAP, owners), f32)],
        axis=0,
    )
    grad_s[...] = folded(sums.T).reshape(grad_s.shape)
    copies = exchange(n_z, z_peer, sem_z.at[2], lambda o: grad_s.at[o], grad_y.at[my_z])
    grad_y[my_z] = grad_s[my_z]
    finish(copies)
    low_z = lax.broadcasted_iota(jnp.int32, (half_z, 128), 1) < 64
    for c in range(half_c):
        lines = grad_y[:, c, :]
        other = swapped(lines)
        grad_x[c] = jnp.where(low_z, lines[:half_z], other[half_z:])
        grad_x[half_c + c] = jnp.where(low_z, other[:half_z], lines[half_z:])
    copies = exchange(
        n_c * n_view, cv_peer, sem_g.at[1], lambda o: grad_x.at[o], grad_u.at[my_view, my_c]
    )
    grad_u[my_view, my_c] = grad_x[my_c]
    _, pullback = jax.vjp(lambda vals: project(vals, camcols), row_vals)
    finish(copies)
    for v in range(n_view):
        turned = unfolded(grad_u[v].reshape(n_src // 2, 128)).T
        for c in range(CAP):
            cot_s[v * CAP + c] = turned[c * 16 : (c + 1) * 16]
    (grads,) = pullback([cot_s[:, index, :] for index in range(ATTRS)])
    for row, value in enumerate(grads):
        all_s[row] = value
    total = jnp.zeros((3 * width, g_dev), f32)
    for v in range(n_view):
        line = jnp.concatenate([all_s[:, v * CAP + c, :] for c in range(CAP)], axis=1)
        total = total + dot(pieces(line), hot_s[v], ((1,), (1,)))
    out_ref[...] = joined(total)


def on_device(params, lists, tile_pos, cam_index, cams, targets):
    owners = lax.axis_size("gauss")
    n_view = lax.axis_size("view")
    n_c = max(2, owners // 16)
    n_z = owners // n_c
    width, g_dev = params.shape
    n_tiles, slots = lists.shape
    half = targets.shape[2] // 2
    rows_c = cams.shape[0]
    f32, bf16 = jnp.float32, jnp.bfloat16
    vmem = pl.BlockSpec(memory_space=pltpu.VMEM)
    plane = (slots, 2 * n_tiles, half)
    shapes = [
        ((n_z, 1, slots), f32),
        ((n_z, 1, slots), f32),
        ((n_z // 4, slots), f32),
        ((n_view, n_c, n_z // 4, slots), f32),
        ((8, 16, owners), f32),
        ((n_c, n_z // 2, 128), f32),
        ((n_c, n_z // 2, 128), f32),
        ((n_z, n_c // 2, 128), f32),
        ((n_z, n_c // 2, 128), f32),
        ((width, CAP, owners), f32),
        ((rows_c, CAP, owners), f32),
        ((width, n_view * CAP, owners), f32),
        ((rows_c, n_view * CAP, owners), f32),
        ((16, n_tiles, slots), f32),
        ((n_z, n_c // 2, 128), f32),
        ((n_z, n_c // 2, 128), f32),
        ((n_c, n_z // 2, 128), f32),
        ((n_view, n_c, n_z // 2, 128), f32),
        ((n_view * CAP, 16, owners), f32),
        ((n_view, g_dev, CAP * owners), bf16),
        ((CAP * owners, n_tiles * slots), bf16),
        (plane, f32),
        (plane, f32),
        (plane, f32),
        (plane, f32),
        (plane, f32),
        ((3,) + plane, f32),
    ]
    return pl.pallas_call(
        lambda *refs: step_kernel(n_view, n_z, n_c, *refs),
        out_shape=(
            jax.ShapeDtypeStruct(targets.shape, f32),
            jax.ShapeDtypeStruct((width, g_dev), f32),
        ),
        in_specs=[pl.BlockSpec(memory_space=pl.ANY)] * 6,
        out_specs=(vmem, vmem),
        scratch_shapes=[
            pltpu.VMEM(params.shape, params.dtype),
            pltpu.VMEM(lists.shape, lists.dtype),
            pltpu.SMEM(tile_pos.shape, tile_pos.dtype),
            pltpu.SMEM(cam_index.shape, cam_index.dtype),
            pltpu.VMEM(cams.shape[::-1], cams.dtype),
            pltpu.VMEM(targets.shape, targets.dtype),
            pltpu.SemaphoreType.DMA((6,)),
        ]
        + [pltpu.VMEM(shape, dtype) for shape, dtype in shapes]
        + [
            pltpu.SemaphoreType.DMA((3, 2, n_z - 1)),
            pltpu.SemaphoreType.DMA((2, n_c - 1)),
            pltpu.SemaphoreType.DMA((2, 2, n_c * n_view - 1)),
        ],
        compiler_params=pltpu.CompilerParams(collective_id=0, has_side_effects=True),
    )(params, lists, tile_pos, cam_index, cams.T, targets)


def solution(mesh):
    return jax.shard_map(
        on_device,
        mesh=mesh,
        in_specs=(
            P(None, "gauss"),
            P(("gauss", "view"), None),
            P(("gauss", "view")),
            P(("gauss", "view")),
            P(),
            P(None, ("gauss", "view"), None),
        ),
        out_specs=(P(None, ("gauss", "view"), None), P(None, "gauss")),
        check_vma=False,
    )
```

```python
import jax
import jax.numpy as jnp
from jax import lax
from jax.experimental import pallas as pl
from jax.experimental.pallas import tpu as pltpu
from jax.sharding import PartitionSpec as P

WIN = 16


def sh_terms(dir_x, dir_y, dir_z):
    return [
        jnp.ones_like(dir_x),
        dir_x,
        dir_y,
        dir_z,
        dir_x * dir_y,
        dir_y * dir_z,
        dir_x * dir_z,
        dir_x * dir_x - dir_y * dir_y,
        3.0 * dir_z * dir_z - 1.0,
        dir_x * (dir_x * dir_x - 3.0 * dir_y * dir_y),
        dir_x * dir_y * dir_z,
        dir_y * (3.0 * dir_x * dir_x - dir_y * dir_y),
        dir_z * (dir_x * dir_x - dir_y * dir_y),
        dir_x * (5.0 * dir_z * dir_z - 1.0),
        dir_y * (5.0 * dir_z * dir_z - 1.0),
        dir_z * (5.0 * dir_z * dir_z - 3.0),
    ]


def project(row_vals, camcols):
    mean_x, mean_y, mean_z = (row_vals[0], row_vals[1], row_vals[2])
    cam_rot = [camcols[index] for index in range(9)]
    focal = camcols[12]
    cam_x = cam_rot[0] * mean_x + cam_rot[1] * mean_y + cam_rot[2] * mean_z + camcols[9]
    cam_y = cam_rot[3] * mean_x + cam_rot[4] * mean_y + cam_rot[5] * mean_z + camcols[10]
    cam_z = cam_rot[6] * mean_x + cam_rot[7] * mean_y + cam_rot[8] * mean_z + camcols[11]
    inv_z = 1.0 / cam_z
    quaternion = row_vals[6:10]
    q_norm = jnp.sqrt(
        quaternion[0] * quaternion[0]
        + quaternion[1] * quaternion[1]
        + quaternion[2] * quaternion[2]
        + quaternion[3] * quaternion[3]
    )
    unit_w = quaternion[0] / q_norm
    unit_x = quaternion[1] / q_norm
    unit_y = quaternion[2] / q_norm
    unit_z = quaternion[3] / q_norm
    rotation = [
        [
            1.0 - 2.0 * (unit_y * unit_y + unit_z * unit_z),
            2.0 * (unit_x * unit_y - unit_w * unit_z),
            2.0 * (unit_x * unit_z + unit_w * unit_y),
        ],
        [
            2.0 * (unit_x * unit_y + unit_w * unit_z),
            1.0 - 2.0 * (unit_x * unit_x + unit_z * unit_z),
            2.0 * (unit_y * unit_z - unit_w * unit_x),
        ],
        [
            2.0 * (unit_x * unit_z - unit_w * unit_y),
            2.0 * (unit_y * unit_z + unit_w * unit_x),
            1.0 - 2.0 * (unit_x * unit_x + unit_y * unit_y),
        ],
    ]
    mixed = [
        [
            cam_rot[3 * row_i] * rotation[0][col_k]
            + cam_rot[3 * row_i + 1] * rotation[1][col_k]
            + cam_rot[3 * row_i + 2] * rotation[2][col_k]
            for col_k in range(3)
        ]
        for row_i in range(3)
    ]
    jac_scale = focal * inv_z
    proj_u = [
        jac_scale * mixed[0][col_k] - jac_scale * cam_x * inv_z * mixed[2][col_k]
        for col_k in range(3)
    ]
    proj_v = [
        jac_scale * mixed[1][col_k] - jac_scale * cam_y * inv_z * mixed[2][col_k]
        for col_k in range(3)
    ]
    var_diag = [jnp.exp(2.0 * row_vals[axis]) for axis in range(3, 6)]
    cov_a = (
        proj_u[0] * proj_u[0] * var_diag[0]
        + proj_u[1] * proj_u[1] * var_diag[1]
        + proj_u[2] * proj_u[2] * var_diag[2]
        + 0.3
    )
    cov_b = (
        proj_u[0] * proj_v[0] * var_diag[0]
        + proj_u[1] * proj_v[1] * var_diag[1]
        + proj_u[2] * proj_v[2] * var_diag[2]
    )
    cov_c = (
        proj_v[0] * proj_v[0] * var_diag[0]
        + proj_v[1] * proj_v[1] * var_diag[1]
        + proj_v[2] * proj_v[2] * var_diag[2]
        + 0.3
    )
    determinant = cov_a * cov_c - cov_b * cov_b
    opacity = jax.nn.sigmoid(row_vals[10])
    distance = jnp.sqrt(cam_x * cam_x + cam_y * cam_y + cam_z * cam_z)
    terms = sh_terms(cam_x / distance, cam_y / distance, cam_z / distance)
    colors = []
    for chan in range(3):
        shade = 0.5 + sum(
            (row_vals[11 + 16 * chan + basis_b] * terms[basis_b] for basis_b in range(16))
        )
        shade = shade + sum(
            (row_vals[59 + feat_j] * camcols[13 + 3 * feat_j + chan] for feat_j in range(5))
        )
        colors.append(shade)
    centre_u = focal * cam_x * inv_z
    centre_v = focal * cam_y * inv_z
    return [
        centre_u,
            centre_v,
            cov_c / determinant,
            -cov_b / determinant,
            cov_a / determinant,
            opacity,
            colors[0],
            colors[1],
            colors[2],
    ]


def tile_values(scalars, shape):
    tile = lax.broadcasted_iota(jnp.int32, shape, 0) % len(scalars)
    out = jnp.full(shape, scalars[0])
    for index, value in enumerate(scalars[1:], 1):
        out = jnp.where(tile == index, value, out)
    return out


CAP = 4
ATTRS = 9


def render_tiles(
    attr_ref, pos_ref, target_ref, picture_ref,
    dx_s, dy_s, exp_s, alpha_s, trans_s, color_s,
):
    n_tiles, slots = attr_ref.shape[1:]
    half = target_ref.shape[2] // 2
    wide = (2 * n_tiles, half)
    attrs = [attr_ref[row] for row in range(ATTRS)]
    attrs8 = [jnp.concatenate([a, a], axis=0) for a in attrs]

    row_id = lax.broadcasted_iota(jnp.int32, wide, 0)
    lane = lax.broadcasted_iota(jnp.int32, wide, 1)
    pixel = lane + jnp.where(row_id >= n_tiles, half, 0)
    base_x = tile_values([16 * (pos_ref[t] % WIN - WIN // 2) for t in range(n_tiles)], wide)
    base_y = tile_values([16 * (pos_ref[t] // WIN - WIN // 2) for t in range(n_tiles)], wide)
    pixel_x = (base_x + pixel % 16).astype(jnp.float32) + 0.5
    pixel_y = (base_y + pixel // 16).astype(jnp.float32) + 0.5

    def spread(values, slot):
        at = jnp.full(wide, slot, jnp.int32)
        return jnp.take_along_axis(values, at, axis=1, mode="promise_in_bounds")

    unroll = 16

    def forward(step, carry):
        trans, r0, r1, r2 = carry
        for inner in range(unroll):
            slot = step * unroll + inner
            u, v, ca, cb, cc, op, c0, c1, c2 = [spread(a, slot) for a in attrs8]
            dx = pixel_x - u
            dy = pixel_y - v
            power = -0.5 * (ca * dx * dx + 2.0 * cb * dx * dy + cc * dy * dy)
            e = jnp.exp(power)
            alpha = op * e
            dx_s[slot] = dx
            dy_s[slot] = dy
            exp_s[slot] = e
            alpha_s[slot] = alpha
            trans_s[slot] = trans
            color_s[0, slot] = c0
            color_s[1, slot] = c1
            color_s[2, slot] = c2
            w = alpha * trans
            r0, r1, r2 = r0 + c0 * w, r1 + c1 * w, r2 + c2 * w
            trans = trans * (1.0 - alpha)
        return trans, r0, r1, r2

    zero = jnp.zeros(wide, jnp.float32)
    _, r0, r1, r2 = lax.fori_loop(
        0, slots // unroll, forward, (jnp.ones(wide, jnp.float32), zero, zero, zero)
    )
    res = []
    for chan, pic in enumerate((r0, r1, r2)):
        picture_ref[chan, :, :half] = pic[:n_tiles]
        picture_ref[chan, :, half:] = pic[n_tiles:]
        want = target_ref[chan]
        res.append(pic - jnp.concatenate([want[:, :half], want[:, half:]], axis=0))

    def backward(step, carry):
        behind, accs = carry
        accs = list(accs)
        for inner in range(unroll):
            slot = slots - 1 - (step * unroll + inner)
            dx, dy, e, alpha, trans = dx_s[slot], dy_s[slot], exp_s[slot], alpha_s[slot], trans_s[slot]
            q = color_s[0, slot] * res[0] + color_s[1, slot] * res[1] + color_s[2, slot] * res[2]
            w = alpha * trans
            diff = q - behind
            gain = trans * diff * e
            behind = behind + alpha * diff
            gx = gain * dx
            gy = gain * dy
            terms = [gain, gx, gy, gx * dx, gx * dy, gy * dy, w * res[0], w * res[1], w * res[2]]
            here = lane == slot
            for index, term in enumerate(terms):
                total = jnp.sum(term, axis=1, keepdims=True)
                accs[index] = jnp.where(here, total, accs[index])
        return behind, tuple(accs)

    _, accs = lax.fori_loop(0, slots // unroll, backward, (zero, (zero,) * 9))
    g0, gx, gy, gxx, gxy, gyy, k0, k1, k2 = [a[:n_tiles] + a[n_tiles:] for a in accs]
    op = attrs[5]
    ca, cb, cc = attrs[2:5]
    cot = [
        op * (ca * gx + cb * gy),
        op * (cb * gx + cc * gy),
        -0.5 * (op * gxx),
        -(op * gxy),
        -0.5 * (op * gyy),
        g0,
        k0,
        k1,
        k2,
    ]
    for row, value in enumerate(cot):
        attr_ref[row] = value


def pieces(values):
    out = []
    for _ in range(3):
        out.append(values.astype(jnp.bfloat16))
        values = values - out[-1].astype(jnp.float32)
    return jnp.concatenate(out, axis=0)


def two_pieces(values):
    high = values.astype(jnp.bfloat16)
    return high, (values - high.astype(jnp.float32)).astype(jnp.bfloat16)


def swapped(values):
    return pltpu.roll(values, 64, axis=1)


def folded(values):
    count = values.shape[0] // 2
    return values[:count] + swapped(values[count:])


def unfolded(values):
    return jnp.concatenate([values, swapped(values)], axis=0)


def joined(values):
    third = values.shape[0] // 3
    return values[:third] + values[third : 2 * third] + values[2 * third :]


def dot(a, b, dims):
    return lax.dot_general(a, b, (dims, ((), ())), preferred_element_type=jnp.float32)


def step_kernel(
    n_view, n_z, n_c,
    params_hbm, ids_hbm, pos_hbm, cam_hbm, cams_hbm, target_hbm,
    picture_ref, out_ref,
    params_ref, ids_ref, pos_ref, cam_ref, cams_ref, target_ref, sem_in,
    want_s, ask_a, ask_p, ask_b, par_t, par_x, par_y, par_s, par_q, own_s, cam_s, all_s, all_cam_s,
    attr_s, grad_s, grad_y, grad_x, grad_u, cot_s, hot_s, pick_s,
    dx_s, dy_s, exp_s, alpha_s, trans_s, color_s,
    sem_z, sem_c, sem_g,
):
    owners = n_z * n_c
    width, g_dev = params_ref.shape
    n_tiles, slots = ids_ref.shape
    f32, bf16 = jnp.float32, jnp.bfloat16
    me = lax.axis_index("gauss")
    my_view = lax.axis_index("view")
    my_z, my_c = me // n_c, lax.rem(me, n_c)

    def z_peer(step):
        other = lax.rem(my_z + step, n_z)
        return other, {"gauss": other * n_c + my_c}

    def cv_peer(step):
        other = lax.rem(my_c + step % n_c, n_c)
        return other, {
            "gauss": my_z * n_c + other,
            "view": lax.rem(my_view + step // n_c, n_view),
        }

    barrier = pltpu.get_barrier_semaphore()
    for count, peer in ((n_z, z_peer), (n_c * n_view, cv_peer)):
        for step in range(1, count):
            pl.semaphore_signal(
                barrier, inc=1, device_id=peer(step)[1], device_id_type=pl.DeviceIdType.MESH
            )

    loads = [
        pltpu.make_async_copy(source, target, sem_in.at[index])
        for index, (source, target) in enumerate(
            (
                (ids_hbm, ids_ref),
                (cam_hbm, cam_ref),
                (params_hbm, params_ref),
                (cams_hbm, cams_ref),
                (pos_hbm, pos_ref),
                (target_hbm, target_ref),
            )
        )
    ]
    for load in loads:
        load.start()

    def exchange(count, peer, sems, source, target):
        copies = []
        for step in range(1, count):
            other, device = peer(step)
            copy = pltpu.make_async_remote_copy(
                src_ref=source(other),
                dst_ref=target,
                send_sem=sems.at[0, step - 1],
                recv_sem=sems.at[1, step - 1],
                device_id=device,
                device_id_type=pl.DeviceIdType.MESH,
            )
            copy.start()
            copies.append(copy)
        return copies

    def finish(copies):
        for copy in copies:
            copy.wait()

    bits = g_dev.bit_length() - 1
    base = 2 * g_dev
    half_c, half_z, n_q = n_c // 2, n_z // 2, n_z // 4
    row = lax.broadcasted_iota(jnp.int32, (owners, slots), 0)
    row_z = lax.rem(row // half_c, n_z)
    row_c = row // (n_z * half_c) * half_c + lax.rem(row, half_c)
    own_row = row_z * n_c + row_c
    lane = lax.broadcasted_iota(jnp.int32, (owners, slots), 1)
    before = (
        lax.broadcasted_iota(jnp.int32, (slots, slots), 0)
        < lax.broadcasted_iota(jnp.int32, (slots, slots), 1)
    )
    before = jnp.where(before, 1.0, 0.0).astype(bf16)
    seen = jnp.zeros((owners, 1), f32)
    loads[0].wait()
    loads[1].wait()
    asked = [jnp.zeros((owners, slots), f32) for _ in range(CAP)]
    for t in range(n_tiles):
        ids = ids_ref[t : t + 1, :]
        owner = lax.shift_right_arithmetic(ids, bits)
        code = (lax.bitwise_and(ids, g_dev - 1) + (1 + base * cam_ref[t])).astype(f32)
        named = own_row == owner
        named_f = jnp.where(named, 1.0, 0.0)
        rank = dot(named_f.astype(bf16), before, ((1,), (0,))) + seen
        seen = seen + jnp.sum(named_f, axis=1, keepdims=True)
        for c in range(CAP):
            chosen = jnp.where(rank == float(c), named_f, 0.0)
            pick_s[c * owners : (c + 1) * owners, t * slots : (t + 1) * slots] = chosen.astype(bf16)
            asked[c] = asked[c] + chosen * code
    spread = jnp.zeros((owners, slots), f32)
    for c in range(CAP):
        column = jnp.sum(asked[c], axis=1, keepdims=True)
        spread = spread + jnp.where(
            lane == my_z // n_q * 32 + row_c * CAP + c, column, 0.0
        )
    spread = spread[: owners // 2] + spread[owners // 2 :]
    same = lax.broadcasted_iota(jnp.int32, (n_z, owners // 2), 0) == (
        lax.broadcasted_iota(jnp.int32, (n_z, owners // 2), 1) // half_c
    )
    same = jnp.where(same, 1.0, 0.0).astype(bf16)
    want = sum(dot(same, part, ((1,), (0,))) for part in two_pieces(spread))
    for z in range(n_z):
        want_s[z] = want[z : z + 1]
    par_t[...] = jnp.zeros(par_t.shape, f32)
    pl.semaphore_wait(barrier, n_z + n_c * n_view - 2)

    copies = exchange(n_z, z_peer, sem_z.at[0], lambda o: want_s.at[o], ask_a.at[my_z])
    ask_a[my_z] = want_s[my_z]
    finish(copies)
    asked = ask_a[...].reshape(n_z, slots)
    packed = asked[:n_q]
    for part in range(1, 4):
        packed = packed + asked[part * n_q : (part + 1) * n_q]
    ask_p[...] = packed
    asking = exchange(
        n_c * n_view, cv_peer, sem_g.at[0], lambda o: ask_p, ask_b.at[my_view, my_c]
    )
    ask_b[my_view, my_c] = packed
    finish(asking[: n_c - 1])

    loads[2].wait()
    loads[3].wait()
    params = params_ref[...]
    cams3 = pieces(cams_ref[...].T)
    n_src = n_z * n_c
    place = lax.broadcasted_iota(jnp.int32, (g_dev, n_src), 0) + 1
    camera = lax.broadcasted_iota(jnp.int32, (cams_ref.shape[0], n_src), 0)
    row32 = lax.broadcasted_iota(jnp.int32, (32, slots), 0)
    lane32 = lax.broadcasted_iota(jnp.int32, (32, slots), 1)
    mine32 = lane32 == row32 // 8 * 32 + my_c * CAP + lax.rem(row32, 8)
    mine32 = jnp.where(mine32, 1.0, 0.0).astype(bf16)
    line_no = lax.broadcasted_iota(jnp.int32, (n_c * n_q, n_src), 0)
    src = lax.broadcasted_iota(jnp.int32, (n_c * n_q, n_src), 1)
    src_z = src // (n_c * half_z) * half_z + lax.rem(src, half_z)
    src_line = lax.rem(src // half_z, n_c) * n_q + lax.rem(src_z, n_q)
    orders = [
        jnp.where((line_no == src_line) & (src_z // n_q == part), 1.0, 0.0).astype(bf16)
        for part in range(4)
    ]

    def look_up(view, rows_ref, cams_out, hot_ref, first):
        lines = jnp.concatenate([ask_b[view, c] for c in range(n_c)], axis=0)
        found = sum(dot(mine32, part, ((1,), (1,))) for part in two_pieces(lines))
        codes = jnp.zeros((8, n_src), f32)
        for index, order in enumerate(orders):
            for part in two_pieces(found[index * 8 : (index + 1) * 8]):
                codes = codes + dot(part, order, ((1,), (0,)))
        codes = codes.astype(jnp.int32)
        index = lax.bitwise_and(codes, base - 1)
        seen_by = lax.shift_right_logical(codes, bits + 1)
        for c in range(CAP):
            hot = jnp.where(place == index[c : c + 1], 1.0, 0.0).astype(bf16)
            if hot_ref is not None:
                hot_ref[:, c * n_src : (c + 1) * n_src] = hot
            rows_ref[:, first + c, :] = dot(params, hot, ((1,), (0,)))
            chosen = jnp.where(camera == seen_by[c : c + 1], 1.0, 0.0).astype(bf16)
            cams_out[:, first + c, :] = joined(dot(cams3, chosen, ((1,), (0,))))
        return index[:CAP] > 0

    def safe(rows_ref, cams_in, live):
        row_vals = [rows_ref[row] for row in range(width)]
        row_vals[6] = jnp.where(live, row_vals[6], 1.0)
        camcols = [cams_in[row] for row in range(cams_ref.shape[1])]
        camcols[11] = jnp.where(live, camcols[11], 4.0)
        return row_vals, camcols

    live = look_up(my_view, own_s, cam_s, None, 0)
    row_vals, camcols = safe(own_s, cam_s, live)
    for index, value in enumerate(project(row_vals, camcols)):
        par_t[:CAP, index, :] = value
    par_x[...] = folded(par_t[...].reshape(8 * 16, n_src).T).reshape(par_x.shape)

    copies = exchange(n_c, cv_peer, sem_c, lambda o: par_x.at[o], par_y.at[my_c])
    par_y[my_c] = par_x[my_c]
    finish(copies)
    low_c = lax.broadcasted_iota(jnp.int32, (half_c, 128), 1) < 64
    for z in range(half_z):
        lines = par_y[:, z, :]
        other = swapped(lines)
        par_s[z] = jnp.where(low_c, lines[:half_c], other[half_c:])
        par_s[half_z + z] = jnp.where(low_c, other[:half_c], lines[half_c:])
    copies = exchange(n_z, z_peer, sem_z.at[1], lambda o: par_s.at[o], par_q.at[my_z])
    par_q[my_z] = par_s[my_z]

    finish(asking[n_c - 1 :])
    lives = [
        look_up(v, all_s, all_cam_s, hot_s.at[v], v * CAP) for v in range(n_view)
    ]
    all_live = jnp.concatenate([jnp.where(a, 1.0, 0.0) for a in lives], axis=0) > 0.5
    row_vals, camcols = safe(all_s, all_cam_s, all_live)
    finish(copies)

    turned = unfolded(par_q[...].reshape(owners // 2, 128)).T
    left = jnp.concatenate([pieces(turned[c * 16 : (c + 1) * 16]) for c in range(CAP)], axis=1)
    found = joined(dot(left, pick_s[...], ((1,), (0,))))
    for t in range(n_tiles):
        attr_s[:, t, :] = found[:, t * slots : (t + 1) * slots]

    loads[4].wait()
    loads[5].wait()
    render_tiles(
        attr_s, pos_ref, target_ref, picture_ref,
        dx_s, dy_s, exp_s, alpha_s, trans_s, color_s,
    )

    grads = jnp.concatenate([attr_s[:, t, :] for t in range(n_tiles)], axis=1)
    sums = joined(dot(pieces(grads), pick_s[...], ((1,), (1,))))
    sums = jnp.concatenate(
        [sums[:, c * owners : (c + 1) * owners] for c in range(CAP)]
        + [jnp.zeros((128 - 16 * CAP, owners), f32)],
        axis=0,
    )
    grad_s[...] = folded(sums.T).reshape(grad_s.shape)
    copies = exchange(n_z, z_peer, sem_z.at[2], lambda o: grad_s.at[o], grad_y.at[my_z])
    grad_y[my_z] = grad_s[my_z]
    finish(copies)
    low_z = lax.broadcasted_iota(jnp.int32, (half_z, 128), 1) < 64
    for c in range(half_c):
        lines = grad_y[:, c, :]
        other = swapped(lines)
        grad_x[c] = jnp.where(low_z, lines[:half_z], other[half_z:])
        grad_x[half_c + c] = jnp.where(low_z, other[:half_z], lines[half_z:])
    copies = exchange(
        n_c * n_view, cv_peer, sem_g.at[1], lambda o: grad_x.at[o], grad_u.at[my_view, my_c]
    )
    grad_u[my_view, my_c] = grad_x[my_c]
    _, pullback = jax.vjp(lambda vals: project(vals, camcols), row_vals)
    finish(copies)
    for v in range(n_view):
        turned = unfolded(grad_u[v].reshape(n_src // 2, 128)).T
        for c in range(CAP):
            cot_s[v * CAP + c] = turned[c * 16 : (c + 1) * 16]
    (grads,) = pullback([cot_s[:, index, :] for index in range(ATTRS)])
    for row, value in enumerate(grads):
        all_s[row] = value
    total = jnp.zeros((3 * width, g_dev), f32)
    for v in range(n_view):
        line = jnp.concatenate([all_s[:, v * CAP + c, :] for c in range(CAP)], axis=1)
        total = total + dot(pieces(line), hot_s[v], ((1,), (1,)))
    out_ref[...] = joined(total)


def on_device(params, lists, tile_pos, cam_index, cams, targets):
    owners = lax.axis_size("gauss")
    n_view = lax.axis_size("view")
    n_c = max(2, owners // 16)
    n_z = owners // n_c
    width, g_dev = params.shape
    n_tiles, slots = lists.shape
    half = targets.shape[2] // 2
    rows_c = cams.shape[0]
    f32, bf16 = jnp.float32, jnp.bfloat16
    vmem = pl.BlockSpec(memory_space=pltpu.VMEM)
    plane = (slots, 2 * n_tiles, half)
    shapes = [
        ((n_z, 1, slots), f32),
        ((n_z, 1, slots), f32),
        ((n_z // 4, slots), f32),
        ((n_view, n_c, n_z // 4, slots), f32),
        ((8, 16, owners), f32),
        ((n_c, n_z // 2, 128), f32),
        ((n_c, n_z // 2, 128), f32),
        ((n_z, n_c // 2, 128), f32),
        ((n_z, n_c // 2, 128), f32),
        ((width, CAP, owners), f32),
        ((rows_c, CAP, owners), f32),
        ((width, n_view * CAP, owners), f32),
        ((rows_c, n_view * CAP, owners), f32),
        ((16, n_tiles, slots), f32),
        ((n_z, n_c // 2, 128), f32),
        ((n_z, n_c // 2, 128), f32),
        ((n_c, n_z // 2, 128), f32),
        ((n_view, n_c, n_z // 2, 128), f32),
        ((n_view * CAP, 16, owners), f32),
        ((n_view, g_dev, CAP * owners), bf16),
        ((CAP * owners, n_tiles * slots), bf16),
        (plane, f32),
        (plane, f32),
        (plane, f32),
        (plane, f32),
        (plane, f32),
        ((3,) + plane, f32),
    ]
    return pl.pallas_call(
        lambda *refs: step_kernel(n_view, n_z, n_c, *refs),
        out_shape=(
            pltpu.VMEM(targets.shape, f32),
            pltpu.VMEM((width, g_dev), f32),
        ),
        in_specs=[pl.BlockSpec(memory_space=pl.ANY)] * 6,
        out_specs=(vmem, vmem),
        scratch_shapes=[
            pltpu.VMEM(params.shape, params.dtype),
            pltpu.VMEM(lists.shape, lists.dtype),
            pltpu.SMEM(tile_pos.shape, tile_pos.dtype),
            pltpu.SMEM(cam_index.shape, cam_index.dtype),
            pltpu.VMEM(cams.shape[::-1], cams.dtype),
            pltpu.VMEM(targets.shape, targets.dtype),
            pltpu.SemaphoreType.DMA((6,)),
        ]
        + [pltpu.VMEM(shape, dtype) for shape, dtype in shapes]
        + [
            pltpu.SemaphoreType.DMA((3, 2, n_z - 1)),
            pltpu.SemaphoreType.DMA((2, n_c - 1)),
            pltpu.SemaphoreType.DMA((2, 2, n_c * n_view - 1)),
        ],
        compiler_params=pltpu.CompilerParams(collective_id=0, has_side_effects=True),
    )(params, lists, tile_pos, cam_index, cams.T, targets)


def solution(mesh):
    return jax.shard_map(
        on_device,
        mesh=mesh,
        in_specs=(
            P(None, "gauss"),
            P(("gauss", "view"), None),
            P(("gauss", "view")),
            P(("gauss", "view")),
            P(),
            P(None, ("gauss", "view"), None),
        ),
        out_specs=(P(None, ("gauss", "view"), None), P(None, "gauss")),
        check_vma=False,
    )
```

```python
import jax
import jax.numpy as jnp
from jax import lax
from jax.experimental import pallas as pl
from jax.experimental.pallas import tpu as pltpu
from jax.sharding import PartitionSpec as P

WIN = 16


def sh_terms(dir_x, dir_y, dir_z):
    return [
        jnp.ones_like(dir_x),
        dir_x,
        dir_y,
        dir_z,
        dir_x * dir_y,
        dir_y * dir_z,
        dir_x * dir_z,
        dir_x * dir_x - dir_y * dir_y,
        3.0 * dir_z * dir_z - 1.0,
        dir_x * (dir_x * dir_x - 3.0 * dir_y * dir_y),
        dir_x * dir_y * dir_z,
        dir_y * (3.0 * dir_x * dir_x - dir_y * dir_y),
        dir_z * (dir_x * dir_x - dir_y * dir_y),
        dir_x * (5.0 * dir_z * dir_z - 1.0),
        dir_y * (5.0 * dir_z * dir_z - 1.0),
        dir_z * (5.0 * dir_z * dir_z - 3.0),
    ]


def project(row_vals, camcols):
    mean_x, mean_y, mean_z = (row_vals[0], row_vals[1], row_vals[2])
    cam_rot = [camcols[index] for index in range(9)]
    focal = camcols[12]
    cam_x = cam_rot[0] * mean_x + cam_rot[1] * mean_y + cam_rot[2] * mean_z + camcols[9]
    cam_y = cam_rot[3] * mean_x + cam_rot[4] * mean_y + cam_rot[5] * mean_z + camcols[10]
    cam_z = cam_rot[6] * mean_x + cam_rot[7] * mean_y + cam_rot[8] * mean_z + camcols[11]
    inv_z = 1.0 / cam_z
    quaternion = row_vals[6:10]
    q_norm = jnp.sqrt(
        quaternion[0] * quaternion[0]
        + quaternion[1] * quaternion[1]
        + quaternion[2] * quaternion[2]
        + quaternion[3] * quaternion[3]
    )
    unit_w = quaternion[0] / q_norm
    unit_x = quaternion[1] / q_norm
    unit_y = quaternion[2] / q_norm
    unit_z = quaternion[3] / q_norm
    rotation = [
        [
            1.0 - 2.0 * (unit_y * unit_y + unit_z * unit_z),
            2.0 * (unit_x * unit_y - unit_w * unit_z),
            2.0 * (unit_x * unit_z + unit_w * unit_y),
        ],
        [
            2.0 * (unit_x * unit_y + unit_w * unit_z),
            1.0 - 2.0 * (unit_x * unit_x + unit_z * unit_z),
            2.0 * (unit_y * unit_z - unit_w * unit_x),
        ],
        [
            2.0 * (unit_x * unit_z - unit_w * unit_y),
            2.0 * (unit_y * unit_z + unit_w * unit_x),
            1.0 - 2.0 * (unit_x * unit_x + unit_y * unit_y),
        ],
    ]
    mixed = [
        [
            cam_rot[3 * row_i] * rotation[0][col_k]
            + cam_rot[3 * row_i + 1] * rotation[1][col_k]
            + cam_rot[3 * row_i + 2] * rotation[2][col_k]
            for col_k in range(3)
        ]
        for row_i in range(3)
    ]
    jac_scale = focal * inv_z
    proj_u = [
        jac_scale * mixed[0][col_k] - jac_scale * cam_x * inv_z * mixed[2][col_k]
        for col_k in range(3)
    ]
    proj_v = [
        jac_scale * mixed[1][col_k] - jac_scale * cam_y * inv_z * mixed[2][col_k]
        for col_k in range(3)
    ]
    var_diag = [jnp.exp(2.0 * row_vals[axis]) for axis in range(3, 6)]
    cov_a = (
        proj_u[0] * proj_u[0] * var_diag[0]
        + proj_u[1] * proj_u[1] * var_diag[1]
        + proj_u[2] * proj_u[2] * var_diag[2]
        + 0.3
    )
    cov_b = (
        proj_u[0] * proj_v[0] * var_diag[0]
        + proj_u[1] * proj_v[1] * var_diag[1]
        + proj_u[2] * proj_v[2] * var_diag[2]
    )
    cov_c = (
        proj_v[0] * proj_v[0] * var_diag[0]
        + proj_v[1] * proj_v[1] * var_diag[1]
        + proj_v[2] * proj_v[2] * var_diag[2]
        + 0.3
    )
    determinant = cov_a * cov_c - cov_b * cov_b
    opacity = jax.nn.sigmoid(row_vals[10])
    distance = jnp.sqrt(cam_x * cam_x + cam_y * cam_y + cam_z * cam_z)
    terms = sh_terms(cam_x / distance, cam_y / distance, cam_z / distance)
    colors = []
    for chan in range(3):
        shade = 0.5 + sum(
            (row_vals[11 + 16 * chan + basis_b] * terms[basis_b] for basis_b in range(16))
        )
        shade = shade + sum(
            (row_vals[59 + feat_j] * camcols[13 + 3 * feat_j + chan] for feat_j in range(5))
        )
        colors.append(shade)
    centre_u = focal * cam_x * inv_z
    centre_v = focal * cam_y * inv_z
    return [
        centre_u,
            centre_v,
            cov_c / determinant,
            -cov_b / determinant,
            cov_a / determinant,
            opacity,
            colors[0],
            colors[1],
            colors[2],
    ]


def tile_values(scalars, shape):
    tile = lax.broadcasted_iota(jnp.int32, shape, 0) % len(scalars)
    out = jnp.full(shape, scalars[0])
    for index, value in enumerate(scalars[1:], 1):
        out = jnp.where(tile == index, value, out)
    return out


CAP = 4
ATTRS = 9


def render_tiles(
    attr_ref, pos_ref, target_ref, picture_ref,
    dx_s, dy_s, exp_s, alpha_s, trans_s, color_s,
):
    n_tiles, slots = attr_ref.shape[1:]
    half = target_ref.shape[2] // 2
    wide = (2 * n_tiles, half)
    attrs = [attr_ref[row] for row in range(ATTRS)]
    attrs8 = [jnp.concatenate([a, a], axis=0) for a in attrs]

    row_id = lax.broadcasted_iota(jnp.int32, wide, 0)
    lane = lax.broadcasted_iota(jnp.int32, wide, 1)
    pixel = lane + jnp.where(row_id >= n_tiles, half, 0)
    base_x = tile_values([16 * (pos_ref[t] % WIN - WIN // 2) for t in range(n_tiles)], wide)
    base_y = tile_values([16 * (pos_ref[t] // WIN - WIN // 2) for t in range(n_tiles)], wide)
    pixel_x = (base_x + pixel % 16).astype(jnp.float32) + 0.5
    pixel_y = (base_y + pixel // 16).astype(jnp.float32) + 0.5

    def spread(values, slot):
        at = jnp.full(wide, slot, jnp.int32)
        return jnp.take_along_axis(values, at, axis=1, mode="promise_in_bounds")

    unroll = 16

    def forward(step, carry):
        trans, r0, r1, r2 = carry
        for inner in range(unroll):
            slot = step * unroll + inner
            u, v, ca, cb, cc, op, c0, c1, c2 = [spread(a, slot) for a in attrs8]
            dx = pixel_x - u
            dy = pixel_y - v
            power = -0.5 * (ca * dx * dx + 2.0 * cb * dx * dy + cc * dy * dy)
            e = jnp.exp(power)
            alpha = op * e
            dx_s[slot] = dx
            dy_s[slot] = dy
            exp_s[slot] = e
            alpha_s[slot] = alpha
            trans_s[slot] = trans
            color_s[0, slot] = c0
            color_s[1, slot] = c1
            color_s[2, slot] = c2
            w = alpha * trans
            r0, r1, r2 = r0 + c0 * w, r1 + c1 * w, r2 + c2 * w
            trans = trans * (1.0 - alpha)
        return trans, r0, r1, r2

    zero = jnp.zeros(wide, jnp.float32)
    _, r0, r1, r2 = lax.fori_loop(
        0, slots // unroll, forward, (jnp.ones(wide, jnp.float32), zero, zero, zero)
    )
    res = []
    for chan, pic in enumerate((r0, r1, r2)):
        picture_ref[chan, :, :half] = pic[:n_tiles]
        picture_ref[chan, :, half:] = pic[n_tiles:]
        want = target_ref[chan]
        res.append(pic - jnp.concatenate([want[:, :half], want[:, half:]], axis=0))

    def backward(step, carry):
        behind, accs = carry
        accs = list(accs)
        for inner in range(unroll):
            slot = slots - 1 - (step * unroll + inner)
            dx, dy, e, alpha, trans = dx_s[slot], dy_s[slot], exp_s[slot], alpha_s[slot], trans_s[slot]
            q = color_s[0, slot] * res[0] + color_s[1, slot] * res[1] + color_s[2, slot] * res[2]
            w = alpha * trans
            diff = q - behind
            gain = trans * diff * e
            behind = behind + alpha * diff
            gx = gain * dx
            gy = gain * dy
            terms = [gain, gx, gy, gx * dx, gx * dy, gy * dy, w * res[0], w * res[1], w * res[2]]
            here = lane == slot
            for index, term in enumerate(terms):
                total = jnp.sum(term, axis=1, keepdims=True)
                accs[index] = jnp.where(here, total, accs[index])
        return behind, tuple(accs)

    _, accs = lax.fori_loop(0, slots // unroll, backward, (zero, (zero,) * 9))
    g0, gx, gy, gxx, gxy, gyy, k0, k1, k2 = [a[:n_tiles] + a[n_tiles:] for a in accs]
    op = attrs[5]
    ca, cb, cc = attrs[2:5]
    cot = [
        op * (ca * gx + cb * gy),
        op * (cb * gx + cc * gy),
        -0.5 * (op * gxx),
        -(op * gxy),
        -0.5 * (op * gyy),
        g0,
        k0,
        k1,
        k2,
    ]
    for row, value in enumerate(cot):
        attr_ref[row] = value


def pieces(values):
    out = []
    for _ in range(3):
        out.append(values.astype(jnp.bfloat16))
        values = values - out[-1].astype(jnp.float32)
    return jnp.concatenate(out, axis=0)


def two_pieces(values):
    high = values.astype(jnp.bfloat16)
    return high, (values - high.astype(jnp.float32)).astype(jnp.bfloat16)


def swapped(values):
    return pltpu.roll(values, 64, axis=1)


def folded(values):
    count = values.shape[0] // 2
    return values[:count] + swapped(values[count:])


def unfolded(values):
    return jnp.concatenate([values, swapped(values)], axis=0)


def joined(values):
    third = values.shape[0] // 3
    return values[:third] + values[third : 2 * third] + values[2 * third :]


def dot(a, b, dims):
    return lax.dot_general(a, b, (dims, ((), ())), preferred_element_type=jnp.float32)


def step_kernel(
    n_view, n_z, n_c,
    params_hbm, ids_hbm, pos_hbm, cam_hbm, cams_hbm, target_hbm,
    picture_ref, out_ref,
    params_ref, ids_ref, pos_ref, cam_ref, cams_ref, target_ref, sem_in,
    want_s, ask_a, ask_p, ask_b, par_t, par_x, par_y, par_s, par_q, own_s, cam_s, all_s, all_cam_s,
    attr_s, grad_s, grad_y, grad_x, grad_u, cot_s, hot_s, pick_s,
    dx_s, dy_s, exp_s, alpha_s, trans_s, color_s,
    sem_z, sem_c, sem_g,
):
    owners = n_z * n_c
    width, g_dev = params_ref.shape
    n_tiles, slots = ids_ref.shape
    f32, bf16 = jnp.float32, jnp.bfloat16
    me = lax.axis_index("gauss")
    my_view = lax.axis_index("view")
    my_z, my_c = me // n_c, lax.rem(me, n_c)

    def far_first(count):
        return sorted(range(1, count), key=lambda step: -min(step, count - step))

    def z_peer(step):
        other = lax.rem(my_z + step, n_z)
        return other, {"gauss": other * n_c + my_c}

    def cv_peer(step):
        other = lax.rem(my_c + step % n_c, n_c)
        return other, {
            "gauss": my_z * n_c + other,
            "view": lax.rem(my_view + step // n_c, n_view),
        }

    barrier = pltpu.get_barrier_semaphore()
    for count, peer in ((n_z, z_peer), (n_c * n_view, cv_peer)):
        for step in far_first(count):
            pl.semaphore_signal(
                barrier, inc=1, device_id=peer(step)[1], device_id_type=pl.DeviceIdType.MESH
            )

    loads = [
        pltpu.make_async_copy(source, target, sem_in.at[index])
        for index, (source, target) in enumerate(
            (
                (ids_hbm, ids_ref),
                (cam_hbm, cam_ref),
                (params_hbm, params_ref),
                (cams_hbm, cams_ref),
                (pos_hbm, pos_ref),
                (target_hbm, target_ref),
            )
        )
    ]
    for load in loads:
        load.start()

    def exchange(count, peer, sems, source, target):
        copies = []
        for step in range(1, count):
            other, device = peer(step)
            copy = pltpu.make_async_remote_copy(
                src_ref=source(other),
                dst_ref=target,
                send_sem=sems.at[0, step - 1],
                recv_sem=sems.at[1, step - 1],
                device_id=device,
                device_id_type=pl.DeviceIdType.MESH,
            )
            copies.append(copy)
        for step in far_first(count) if count == n_z else range(1, count):
            copies[step - 1].start()
        return copies

    def finish(copies):
        for copy in copies:
            copy.wait()

    bits = g_dev.bit_length() - 1
    base = 2 * g_dev
    half_c, half_z, n_q = n_c // 2, n_z // 2, n_z // 4
    row = lax.broadcasted_iota(jnp.int32, (owners, slots), 0)
    row_z = lax.rem(row // half_c, n_z)
    row_c = row // (n_z * half_c) * half_c + lax.rem(row, half_c)
    own_row = row_z * n_c + row_c
    lane = lax.broadcasted_iota(jnp.int32, (owners, slots), 1)
    before = (
        lax.broadcasted_iota(jnp.int32, (slots, slots), 0)
        < lax.broadcasted_iota(jnp.int32, (slots, slots), 1)
    )
    before = jnp.where(before, 1.0, 0.0).astype(bf16)
    seen = jnp.zeros((owners, 1), f32)
    loads[0].wait()
    loads[1].wait()
    asked = [jnp.zeros((owners, slots), f32) for _ in range(CAP)]
    for t in range(n_tiles):
        ids = ids_ref[t : t + 1, :]
        owner = lax.shift_right_arithmetic(ids, bits)
        code = (lax.bitwise_and(ids, g_dev - 1) + (1 + base * cam_ref[t])).astype(f32)
        named = own_row == owner
        named_f = jnp.where(named, 1.0, 0.0)
        rank = dot(named_f.astype(bf16), before, ((1,), (0,))) + seen
        seen = seen + jnp.sum(named_f, axis=1, keepdims=True)
        for c in range(CAP):
            chosen = jnp.where(rank == float(c), named_f, 0.0)
            pick_s[c * owners : (c + 1) * owners, t * slots : (t + 1) * slots] = chosen.astype(bf16)
            asked[c] = asked[c] + chosen * code
    spread = jnp.zeros((owners, slots), f32)
    for c in range(CAP):
        column = jnp.sum(asked[c], axis=1, keepdims=True)
        spread = spread + jnp.where(
            lane == my_z // n_q * 32 + row_c * CAP + c, column, 0.0
        )
    spread = spread[: owners // 2] + spread[owners // 2 :]
    same = lax.broadcasted_iota(jnp.int32, (n_z, owners // 2), 0) == (
        lax.broadcasted_iota(jnp.int32, (n_z, owners // 2), 1) // half_c
    )
    same = jnp.where(same, 1.0, 0.0).astype(bf16)
    want = sum(dot(same, part, ((1,), (0,))) for part in two_pieces(spread))
    for z in range(n_z):
        want_s[z] = want[z : z + 1]
    par_t[...] = jnp.zeros(par_t.shape, f32)
    pl.semaphore_wait(barrier, n_z + n_c * n_view - 2)

    copies = exchange(n_z, z_peer, sem_z.at[0], lambda o: want_s.at[o], ask_a.at[my_z])
    ask_a[my_z] = want_s[my_z]
    finish(copies)
    asked = ask_a[...].reshape(n_z, slots)
    packed = asked[:n_q]
    for part in range(1, 4):
        packed = packed + asked[part * n_q : (part + 1) * n_q]
    ask_p[...] = packed
    asking = exchange(
        n_c * n_view, cv_peer, sem_g.at[0], lambda o: ask_p, ask_b.at[my_view, my_c]
    )
    ask_b[my_view, my_c] = packed
    finish(asking[: n_c - 1])

    loads[2].wait()
    loads[3].wait()
    params = params_ref[...]
    cams3 = pieces(cams_ref[...].T)
    n_src = n_z * n_c
    place = lax.broadcasted_iota(jnp.int32, (g_dev, n_src), 0) + 1
    camera = lax.broadcasted_iota(jnp.int32, (cams_ref.shape[0], n_src), 0)
    row32 = lax.broadcasted_iota(jnp.int32, (32, slots), 0)
    lane32 = lax.broadcasted_iota(jnp.int32, (32, slots), 1)
    mine32 = lane32 == row32 // 8 * 32 + my_c * CAP + lax.rem(row32, 8)
    mine32 = jnp.where(mine32, 1.0, 0.0).astype(bf16)
    line_no = lax.broadcasted_iota(jnp.int32, (n_c * n_q, n_src), 0)
    src = lax.broadcasted_iota(jnp.int32, (n_c * n_q, n_src), 1)
    src_z = src // (n_c * half_z) * half_z + lax.rem(src, half_z)
    src_line = lax.rem(src // half_z, n_c) * n_q + lax.rem(src_z, n_q)
    orders = [
        jnp.where((line_no == src_line) & (src_z // n_q == part), 1.0, 0.0).astype(bf16)
        for part in range(4)
    ]

    def look_up(view, rows_ref, cams_out, hot_ref, first):
        lines = jnp.concatenate([ask_b[view, c] for c in range(n_c)], axis=0)
        found = sum(dot(mine32, part, ((1,), (1,))) for part in two_pieces(lines))
        codes = jnp.zeros((8, n_src), f32)
        for index, order in enumerate(orders):
            for part in two_pieces(found[index * 8 : (index + 1) * 8]):
                codes = codes + dot(part, order, ((1,), (0,)))
        codes = codes.astype(jnp.int32)
        index = lax.bitwise_and(codes, base - 1)
        seen_by = lax.shift_right_logical(codes, bits + 1)
        for c in range(CAP):
            hot = jnp.where(place == index[c : c + 1], 1.0, 0.0).astype(bf16)
            if hot_ref is not None:
                hot_ref[:, c * n_src : (c + 1) * n_src] = hot
            rows_ref[:, first + c, :] = dot(params, hot, ((1,), (0,)))
            chosen = jnp.where(camera == seen_by[c : c + 1], 1.0, 0.0).astype(bf16)
            cams_out[:, first + c, :] = joined(dot(cams3, chosen, ((1,), (0,))))
        return index[:CAP] > 0

    def safe(rows_ref, cams_in, live):
        row_vals = [rows_ref[row] for row in range(width)]
        row_vals[6] = jnp.where(live, row_vals[6], 1.0)
        camcols = [cams_in[row] for row in range(cams_ref.shape[1])]
        camcols[11] = jnp.where(live, camcols[11], 4.0)
        return row_vals, camcols

    live = look_up(my_view, own_s, cam_s, None, 0)
    row_vals, camcols = safe(own_s, cam_s, live)
    for index, value in enumerate(project(row_vals, camcols)):
        par_t[:CAP, index, :] = value
    par_x[...] = folded(par_t[...].reshape(8 * 16, n_src).T).reshape(par_x.shape)

    copies = exchange(n_c, cv_peer, sem_c, lambda o: par_x.at[o], par_y.at[my_c])
    par_y[my_c] = par_x[my_c]
    finish(copies)
    low_c = lax.broadcasted_iota(jnp.int32, (half_c, 128), 1) < 64
    for z in range(half_z):
        lines = par_y[:, z, :]
        other = swapped(lines)
        par_s[z] = jnp.where(low_c, lines[:half_c], other[half_c:])
        par_s[half_z + z] = jnp.where(low_c, other[:half_c], lines[half_c:])
    copies = exchange(n_z, z_peer, sem_z.at[1], lambda o: par_s.at[o], par_q.at[my_z])
    par_q[my_z] = par_s[my_z]

    finish(asking[n_c - 1 :])
    lives = [
        look_up(v, all_s, all_cam_s, hot_s.at[v], v * CAP) for v in range(n_view)
    ]
    all_live = jnp.concatenate([jnp.where(a, 1.0, 0.0) for a in lives], axis=0) > 0.5
    row_vals, camcols = safe(all_s, all_cam_s, all_live)
    finish(copies)

    turned = unfolded(par_q[...].reshape(owners // 2, 128)).T
    left = jnp.concatenate([pieces(turned[c * 16 : (c + 1) * 16]) for c in range(CAP)], axis=1)
    found = joined(dot(left, pick_s[...], ((1,), (0,))))
    for t in range(n_tiles):
        attr_s[:, t, :] = found[:, t * slots : (t + 1) * slots]

    loads[4].wait()
    loads[5].wait()
    render_tiles(
        attr_s, pos_ref, target_ref, picture_ref,
        dx_s, dy_s, exp_s, alpha_s, trans_s, color_s,
    )

    grads = jnp.concatenate([attr_s[:, t, :] for t in range(n_tiles)], axis=1)
    sums = joined(dot(pieces(grads), pick_s[...], ((1,), (1,))))
    sums = jnp.concatenate(
        [sums[:, c * owners : (c + 1) * owners] for c in range(CAP)]
        + [jnp.zeros((128 - 16 * CAP, owners), f32)],
        axis=0,
    )
    grad_s[...] = folded(sums.T).reshape(grad_s.shape)
    copies = exchange(n_z, z_peer, sem_z.at[2], lambda o: grad_s.at[o], grad_y.at[my_z])
    grad_y[my_z] = grad_s[my_z]
    finish(copies)
    low_z = lax.broadcasted_iota(jnp.int32, (half_z, 128), 1) < 64
    for c in range(half_c):
        lines = grad_y[:, c, :]
        other = swapped(lines)
        grad_x[c] = jnp.where(low_z, lines[:half_z], other[half_z:])
        grad_x[half_c + c] = jnp.where(low_z, other[:half_z], lines[half_z:])
    copies = exchange(
        n_c * n_view, cv_peer, sem_g.at[1], lambda o: grad_x.at[o], grad_u.at[my_view, my_c]
    )
    grad_u[my_view, my_c] = grad_x[my_c]
    _, pullback = jax.vjp(lambda vals: project(vals, camcols), row_vals)
    for step in sorted(range(n_view), key=lambda step: min(step, n_view - step)):
        finish(copies[max(step * n_c - 1, 0) : (step + 1) * n_c - 1])
        v = lax.rem(my_view + n_view - step, n_view)
        turned = unfolded(grad_u[v].reshape(n_src // 2, 128)).T
        for c in range(CAP):
            cot_s[v * CAP + c] = turned[c * 16 : (c + 1) * 16]
    (grads,) = pullback([cot_s[:, index, :] for index in range(ATTRS)])
    for row, value in enumerate(grads):
        all_s[row] = value
    total = jnp.zeros((3 * width, g_dev), f32)
    for v in range(n_view):
        line = jnp.concatenate([all_s[:, v * CAP + c, :] for c in range(CAP)], axis=1)
        total = total + dot(pieces(line), hot_s[v], ((1,), (1,)))
    out_ref[...] = joined(total)


def on_device(params, lists, tile_pos, cam_index, cams, targets):
    owners = lax.axis_size("gauss")
    n_view = lax.axis_size("view")
    n_c = max(2, owners // 16)
    n_z = owners // n_c
    width, g_dev = params.shape
    n_tiles, slots = lists.shape
    half = targets.shape[2] // 2
    rows_c = cams.shape[0]
    f32, bf16 = jnp.float32, jnp.bfloat16
    vmem = pl.BlockSpec(memory_space=pltpu.VMEM)
    plane = (slots, 2 * n_tiles, half)
    shapes = [
        ((n_z, 1, slots), f32),
        ((n_z, 1, slots), f32),
        ((n_z // 4, slots), f32),
        ((n_view, n_c, n_z // 4, slots), f32),
        ((8, 16, owners), f32),
        ((n_c, n_z // 2, 128), f32),
        ((n_c, n_z // 2, 128), f32),
        ((n_z, n_c // 2, 128), f32),
        ((n_z, n_c // 2, 128), f32),
        ((width, CAP, owners), f32),
        ((rows_c, CAP, owners), f32),
        ((width, n_view * CAP, owners), f32),
        ((rows_c, n_view * CAP, owners), f32),
        ((16, n_tiles, slots), f32),
        ((n_z, n_c // 2, 128), f32),
        ((n_z, n_c // 2, 128), f32),
        ((n_c, n_z // 2, 128), f32),
        ((n_view, n_c, n_z // 2, 128), f32),
        ((n_view * CAP, 16, owners), f32),
        ((n_view, g_dev, CAP * owners), bf16),
        ((CAP * owners, n_tiles * slots), bf16),
        (plane, f32),
        (plane, f32),
        (plane, f32),
        (plane, f32),
        (plane, f32),
        ((3,) + plane, f32),
    ]
    return pl.pallas_call(
        lambda *refs: step_kernel(n_view, n_z, n_c, *refs),
        out_shape=(
            pltpu.VMEM(targets.shape, f32),
            pltpu.VMEM((width, g_dev), f32),
        ),
        in_specs=[pl.BlockSpec(memory_space=pl.ANY)] * 6,
        out_specs=(vmem, vmem),
        scratch_shapes=[
            pltpu.VMEM(params.shape, params.dtype),
            pltpu.VMEM(lists.shape, lists.dtype),
            pltpu.SMEM(tile_pos.shape, tile_pos.dtype),
            pltpu.SMEM(cam_index.shape, cam_index.dtype),
            pltpu.VMEM(cams.shape[::-1], cams.dtype),
            pltpu.VMEM(targets.shape, targets.dtype),
            pltpu.SemaphoreType.DMA((6,)),
        ]
        + [pltpu.VMEM(shape, dtype) for shape, dtype in shapes]
        + [
            pltpu.SemaphoreType.DMA((3, 2, n_z - 1)),
            pltpu.SemaphoreType.DMA((2, n_c - 1)),
            pltpu.SemaphoreType.DMA((2, 2, n_c * n_view - 1)),
        ],
        compiler_params=pltpu.CompilerParams(collective_id=0, has_side_effects=True),
    )(params, lists, tile_pos, cam_index, cams.T, targets)


def solution(mesh):
    return jax.shard_map(
        on_device,
        mesh=mesh,
        in_specs=(
            P(None, "gauss"),
            P(("gauss", "view"), None),
            P(("gauss", "view")),
            P(("gauss", "view")),
            P(),
            P(None, ("gauss", "view"), None),
        ),
        out_specs=(P(None, ("gauss", "view"), None), P(None, "gauss")),
        check_vma=False,
    )
```

```python
import jax
import jax.numpy as jnp
from jax import lax
from jax.experimental import pallas as pl
from jax.experimental.pallas import tpu as pltpu
from jax.sharding import PartitionSpec as P

WIN = 16


def sh_terms(dir_x, dir_y, dir_z):
    return [
        jnp.ones_like(dir_x),
        dir_x,
        dir_y,
        dir_z,
        dir_x * dir_y,
        dir_y * dir_z,
        dir_x * dir_z,
        dir_x * dir_x - dir_y * dir_y,
        3.0 * dir_z * dir_z - 1.0,
        dir_x * (dir_x * dir_x - 3.0 * dir_y * dir_y),
        dir_x * dir_y * dir_z,
        dir_y * (3.0 * dir_x * dir_x - dir_y * dir_y),
        dir_z * (dir_x * dir_x - dir_y * dir_y),
        dir_x * (5.0 * dir_z * dir_z - 1.0),
        dir_y * (5.0 * dir_z * dir_z - 1.0),
        dir_z * (5.0 * dir_z * dir_z - 3.0),
    ]


def project(row_vals, camcols):
    mean_x, mean_y, mean_z = (row_vals[0], row_vals[1], row_vals[2])
    cam_rot = [camcols[index] for index in range(9)]
    focal = camcols[12]
    cam_x = cam_rot[0] * mean_x + cam_rot[1] * mean_y + cam_rot[2] * mean_z + camcols[9]
    cam_y = cam_rot[3] * mean_x + cam_rot[4] * mean_y + cam_rot[5] * mean_z + camcols[10]
    cam_z = cam_rot[6] * mean_x + cam_rot[7] * mean_y + cam_rot[8] * mean_z + camcols[11]
    inv_z = 1.0 / cam_z
    quaternion = row_vals[6:10]
    q_norm = jnp.sqrt(
        quaternion[0] * quaternion[0]
        + quaternion[1] * quaternion[1]
        + quaternion[2] * quaternion[2]
        + quaternion[3] * quaternion[3]
    )
    unit_w = quaternion[0] / q_norm
    unit_x = quaternion[1] / q_norm
    unit_y = quaternion[2] / q_norm
    unit_z = quaternion[3] / q_norm
    rotation = [
        [
            1.0 - 2.0 * (unit_y * unit_y + unit_z * unit_z),
            2.0 * (unit_x * unit_y - unit_w * unit_z),
            2.0 * (unit_x * unit_z + unit_w * unit_y),
        ],
        [
            2.0 * (unit_x * unit_y + unit_w * unit_z),
            1.0 - 2.0 * (unit_x * unit_x + unit_z * unit_z),
            2.0 * (unit_y * unit_z - unit_w * unit_x),
        ],
        [
            2.0 * (unit_x * unit_z - unit_w * unit_y),
            2.0 * (unit_y * unit_z + unit_w * unit_x),
            1.0 - 2.0 * (unit_x * unit_x + unit_y * unit_y),
        ],
    ]
    mixed = [
        [
            cam_rot[3 * row_i] * rotation[0][col_k]
            + cam_rot[3 * row_i + 1] * rotation[1][col_k]
            + cam_rot[3 * row_i + 2] * rotation[2][col_k]
            for col_k in range(3)
        ]
        for row_i in range(3)
    ]
    jac_scale = focal * inv_z
    proj_u = [
        jac_scale * mixed[0][col_k] - jac_scale * cam_x * inv_z * mixed[2][col_k]
        for col_k in range(3)
    ]
    proj_v = [
        jac_scale * mixed[1][col_k] - jac_scale * cam_y * inv_z * mixed[2][col_k]
        for col_k in range(3)
    ]
    var_diag = [jnp.exp(2.0 * row_vals[axis]) for axis in range(3, 6)]
    cov_a = (
        proj_u[0] * proj_u[0] * var_diag[0]
        + proj_u[1] * proj_u[1] * var_diag[1]
        + proj_u[2] * proj_u[2] * var_diag[2]
        + 0.3
    )
    cov_b = (
        proj_u[0] * proj_v[0] * var_diag[0]
        + proj_u[1] * proj_v[1] * var_diag[1]
        + proj_u[2] * proj_v[2] * var_diag[2]
    )
    cov_c = (
        proj_v[0] * proj_v[0] * var_diag[0]
        + proj_v[1] * proj_v[1] * var_diag[1]
        + proj_v[2] * proj_v[2] * var_diag[2]
        + 0.3
    )
    determinant = cov_a * cov_c - cov_b * cov_b
    opacity = jax.nn.sigmoid(row_vals[10])
    distance = jnp.sqrt(cam_x * cam_x + cam_y * cam_y + cam_z * cam_z)
    terms = sh_terms(cam_x / distance, cam_y / distance, cam_z / distance)
    colors = []
    for chan in range(3):
        shade = 0.5 + sum(
            (row_vals[11 + 16 * chan + basis_b] * terms[basis_b] for basis_b in range(16))
        )
        shade = shade + sum(
            (row_vals[59 + feat_j] * camcols[13 + 3 * feat_j + chan] for feat_j in range(5))
        )
        colors.append(shade)
    centre_u = focal * cam_x * inv_z
    centre_v = focal * cam_y * inv_z
    return [
        centre_u,
            centre_v,
            cov_c / determinant,
            -cov_b / determinant,
            cov_a / determinant,
            opacity,
            colors[0],
            colors[1],
            colors[2],
    ]


def tile_values(scalars, shape):
    tile = lax.broadcasted_iota(jnp.int32, shape, 0) % len(scalars)
    out = jnp.full(shape, scalars[0])
    for index, value in enumerate(scalars[1:], 1):
        out = jnp.where(tile == index, value, out)
    return out


CAP = 4
ATTRS = 9


def render_tiles(
    attr_ref, pos_ref, target_ref, picture_ref,
    dx_s, dy_s, exp_s, alpha_s, trans_s, color_s,
):
    n_tiles, slots = attr_ref.shape[1:]
    half = target_ref.shape[2] // 2
    wide = (2 * n_tiles, half)
    attrs = [attr_ref[row] for row in range(ATTRS)]
    attrs8 = [jnp.concatenate([a, a], axis=0) for a in attrs]

    row_id = lax.broadcasted_iota(jnp.int32, wide, 0)
    lane = lax.broadcasted_iota(jnp.int32, wide, 1)
    pixel = lane + jnp.where(row_id >= n_tiles, half, 0)
    base_x = tile_values([16 * (pos_ref[t] % WIN - WIN // 2) for t in range(n_tiles)], wide)
    base_y = tile_values([16 * (pos_ref[t] // WIN - WIN // 2) for t in range(n_tiles)], wide)
    pixel_x = (base_x + pixel % 16).astype(jnp.float32) + 0.5
    pixel_y = (base_y + pixel // 16).astype(jnp.float32) + 0.5

    def spread(values, slot):
        at = jnp.full(wide, slot, jnp.int32)
        return jnp.take_along_axis(values, at, axis=1, mode="promise_in_bounds")

    unroll = 32

    def forward(step, carry):
        trans, r0, r1, r2 = carry
        for inner in range(unroll):
            slot = step * unroll + inner
            u, v, ca, cb, cc, op, c0, c1, c2 = [spread(a, slot) for a in attrs8]
            dx = pixel_x - u
            dy = pixel_y - v
            power = -0.5 * (ca * dx * dx + 2.0 * cb * dx * dy + cc * dy * dy)
            e = jnp.exp(power)
            alpha = op * e
            dx_s[slot] = dx
            dy_s[slot] = dy
            exp_s[slot] = e
            alpha_s[slot] = alpha
            trans_s[slot] = trans
            color_s[0, slot] = c0
            color_s[1, slot] = c1
            color_s[2, slot] = c2
            w = alpha * trans
            r0, r1, r2 = r0 + c0 * w, r1 + c1 * w, r2 + c2 * w
            trans = trans * (1.0 - alpha)
        return trans, r0, r1, r2

    zero = jnp.zeros(wide, jnp.float32)
    _, r0, r1, r2 = lax.fori_loop(
        0, slots // unroll, forward, (jnp.ones(wide, jnp.float32), zero, zero, zero)
    )
    res = []
    for chan, pic in enumerate((r0, r1, r2)):
        picture_ref[chan, :, :half] = pic[:n_tiles]
        picture_ref[chan, :, half:] = pic[n_tiles:]
        want = target_ref[chan]
        res.append(pic - jnp.concatenate([want[:, :half], want[:, half:]], axis=0))

    def backward(step, carry):
        behind, accs = carry
        accs = list(accs)
        for inner in range(unroll):
            slot = slots - 1 - (step * unroll + inner)
            dx, dy, e, alpha, trans = dx_s[slot], dy_s[slot], exp_s[slot], alpha_s[slot], trans_s[slot]
            q = color_s[0, slot] * res[0] + color_s[1, slot] * res[1] + color_s[2, slot] * res[2]
            w = alpha * trans
            diff = q - behind
            gain = trans * diff * e
            behind = behind + alpha * diff
            gx = gain * dx
            gy = gain * dy
            terms = [gain, gx, gy, gx * dx, gx * dy, gy * dy, w * res[0], w * res[1], w * res[2]]
            here = lane == slot
            for index, term in enumerate(terms):
                total = jnp.sum(term, axis=1, keepdims=True)
                accs[index] = jnp.where(here, total, accs[index])
        return behind, tuple(accs)

    _, accs = lax.fori_loop(0, slots // unroll, backward, (zero, (zero,) * 9))
    g0, gx, gy, gxx, gxy, gyy, k0, k1, k2 = [a[:n_tiles] + a[n_tiles:] for a in accs]
    op = attrs[5]
    ca, cb, cc = attrs[2:5]
    cot = [
        op * (ca * gx + cb * gy),
        op * (cb * gx + cc * gy),
        -0.5 * (op * gxx),
        -(op * gxy),
        -0.5 * (op * gyy),
        g0,
        k0,
        k1,
        k2,
    ]
    for row, value in enumerate(cot):
        attr_ref[row] = value


def pieces(values):
    out = []
    for _ in range(3):
        out.append(values.astype(jnp.bfloat16))
        values = values - out[-1].astype(jnp.float32)
    return jnp.concatenate(out, axis=0)


def two_pieces(values):
    high = values.astype(jnp.bfloat16)
    return high, (values - high.astype(jnp.float32)).astype(jnp.bfloat16)


def swapped(values):
    return pltpu.roll(values, 64, axis=1)


def folded(values):
    count = values.shape[0] // 2
    return values[:count] + swapped(values[count:])


def unfolded(values):
    return jnp.concatenate([values, swapped(values)], axis=0)


def joined(values):
    third = values.shape[0] // 3
    return values[:third] + values[third : 2 * third] + values[2 * third :]


def dot(a, b, dims):
    return lax.dot_general(a, b, (dims, ((), ())), preferred_element_type=jnp.float32)


def step_kernel(
    n_view, n_z, n_c,
    params_hbm, ids_hbm, pos_hbm, cam_hbm, cams_hbm, target_hbm,
    picture_ref, out_ref,
    params_ref, ids_ref, pos_ref, cam_ref, cams_ref, target_ref, sem_in,
    want_s, ask_a, ask_p, ask_b, par_t, par_x, par_y, par_s, par_q, own_s, cam_s, all_s, all_cam_s,
    attr_s, grad_s, grad_y, grad_x, grad_u, cot_s, hot_s, pick_s,
    dx_s, dy_s, exp_s, alpha_s, trans_s, color_s,
    sem_z, sem_c, sem_g,
):
    owners = n_z * n_c
    width, g_dev = params_ref.shape
    n_tiles, slots = ids_ref.shape
    f32, bf16 = jnp.float32, jnp.bfloat16
    me = lax.axis_index("gauss")
    my_view = lax.axis_index("view")
    my_z, my_c = me // n_c, lax.rem(me, n_c)

    def z_peer(step):
        other = lax.rem(my_z + step, n_z)
        return other, {"gauss": other * n_c + my_c}

    def cv_peer(step):
        other = lax.rem(my_c + step % n_c, n_c)
        return other, {
            "gauss": my_z * n_c + other,
            "view": lax.rem(my_view + step // n_c, n_view),
        }

    barrier = pltpu.get_barrier_semaphore()
    for count, peer in ((n_z, z_peer), (n_c * n_view, cv_peer)):
        for step in range(1, count):
            pl.semaphore_signal(
                barrier, inc=1, device_id=peer(step)[1], device_id_type=pl.DeviceIdType.MESH
            )

    loads = [
        pltpu.make_async_copy(source, target, sem_in.at[index])
        for index, (source, target) in enumerate(
            (
                (ids_hbm, ids_ref),
                (cam_hbm, cam_ref),
                (params_hbm, params_ref),
                (cams_hbm, cams_ref),
                (pos_hbm, pos_ref),
                (target_hbm, target_ref),
            )
        )
    ]
    for load in loads:
        load.start()

    def exchange(count, peer, sems, source, target):
        copies = []
        for step in range(1, count):
            other, device = peer(step)
            copy = pltpu.make_async_remote_copy(
                src_ref=source(other),
                dst_ref=target,
                send_sem=sems.at[0, step - 1],
                recv_sem=sems.at[1, step - 1],
                device_id=device,
                device_id_type=pl.DeviceIdType.MESH,
            )
            copy.start()
            copies.append(copy)
        return copies

    def finish(copies):
        for copy in copies:
            copy.wait()

    bits = g_dev.bit_length() - 1
    base = 2 * g_dev
    half_c, half_z, n_q = n_c // 2, n_z // 2, n_z // 4
    row = lax.broadcasted_iota(jnp.int32, (owners, slots), 0)
    row_z = lax.rem(row // half_c, n_z)
    row_c = row // (n_z * half_c) * half_c + lax.rem(row, half_c)
    own_row = row_z * n_c + row_c
    lane = lax.broadcasted_iota(jnp.int32, (owners, slots), 1)
    before = (
        lax.broadcasted_iota(jnp.int32, (slots, slots), 0)
        < lax.broadcasted_iota(jnp.int32, (slots, slots), 1)
    )
    before = jnp.where(before, 1.0, 0.0).astype(bf16)
    seen = jnp.zeros((owners, 1), f32)
    loads[0].wait()
    loads[1].wait()
    asked = [jnp.zeros((owners, slots), f32) for _ in range(CAP)]
    for t in range(n_tiles):
        ids = ids_ref[t : t + 1, :]
        owner = lax.shift_right_arithmetic(ids, bits)
        code = (lax.bitwise_and(ids, g_dev - 1) + (1 + base * cam_ref[t])).astype(f32)
        named = own_row == owner
        named_f = jnp.where(named, 1.0, 0.0)
        rank = dot(named_f.astype(bf16), before, ((1,), (0,))) + seen
        seen = seen + jnp.sum(named_f, axis=1, keepdims=True)
        for c in range(CAP):
            chosen = jnp.where(rank == float(c), named_f, 0.0)
            pick_s[c * owners : (c + 1) * owners, t * slots : (t + 1) * slots] = chosen.astype(bf16)
            asked[c] = asked[c] + chosen * code
    spread = jnp.zeros((owners, slots), f32)
    for c in range(CAP):
        column = jnp.sum(asked[c], axis=1, keepdims=True)
        spread = spread + jnp.where(
            lane == my_z // n_q * 32 + row_c * CAP + c, column, 0.0
        )
    spread = spread[: owners // 2] + spread[owners // 2 :]
    same = lax.broadcasted_iota(jnp.int32, (n_z, owners // 2), 0) == (
        lax.broadcasted_iota(jnp.int32, (n_z, owners // 2), 1) // half_c
    )
    same = jnp.where(same, 1.0, 0.0).astype(bf16)
    want = sum(dot(same, part, ((1,), (0,))) for part in two_pieces(spread))
    for z in range(n_z):
        want_s[z] = want[z : z + 1]
    par_t[...] = jnp.zeros(par_t.shape, f32)
    pl.semaphore_wait(barrier, n_z + n_c * n_view - 2)

    copies = exchange(n_z, z_peer, sem_z.at[0], lambda o: want_s.at[o], ask_a.at[my_z])
    ask_a[my_z] = want_s[my_z]
    finish(copies)
    asked = ask_a[...].reshape(n_z, slots)
    packed = asked[:n_q]
    for part in range(1, 4):
        packed = packed + asked[part * n_q : (part + 1) * n_q]
    ask_p[...] = packed
    asking = exchange(
        n_c * n_view, cv_peer, sem_g.at[0], lambda o: ask_p, ask_b.at[my_view, my_c]
    )
    ask_b[my_view, my_c] = packed
    finish(asking[: n_c - 1])

    loads[2].wait()
    loads[3].wait()
    params = params_ref[...]
    cams3 = pieces(cams_ref[...].T)
    n_src = n_z * n_c
    place = lax.broadcasted_iota(jnp.int32, (g_dev, n_src), 0) + 1
    camera = lax.broadcasted_iota(jnp.int32, (cams_ref.shape[0], n_src), 0)
    row32 = lax.broadcasted_iota(jnp.int32, (32, slots), 0)
    lane32 = lax.broadcasted_iota(jnp.int32, (32, slots), 1)
    mine32 = lane32 == row32 // 8 * 32 + my_c * CAP + lax.rem(row32, 8)
    mine32 = jnp.where(mine32, 1.0, 0.0).astype(bf16)
    line_no = lax.broadcasted_iota(jnp.int32, (n_c * n_q, n_src), 0)
    src = lax.broadcasted_iota(jnp.int32, (n_c * n_q, n_src), 1)
    src_z = src // (n_c * half_z) * half_z + lax.rem(src, half_z)
    src_line = lax.rem(src // half_z, n_c) * n_q + lax.rem(src_z, n_q)
    orders = [
        jnp.where((line_no == src_line) & (src_z // n_q == part), 1.0, 0.0).astype(bf16)
        for part in range(4)
    ]

    def look_up(view, rows_ref, cams_out, hot_ref, first):
        lines = jnp.concatenate([ask_b[view, c] for c in range(n_c)], axis=0)
        found = sum(dot(mine32, part, ((1,), (1,))) for part in two_pieces(lines))
        codes = jnp.zeros((8, n_src), f32)
        for index, order in enumerate(orders):
            for part in two_pieces(found[index * 8 : (index + 1) * 8]):
                codes = codes + dot(part, order, ((1,), (0,)))
        codes = codes.astype(jnp.int32)
        index = lax.bitwise_and(codes, base - 1)
        seen_by = lax.shift_right_logical(codes, bits + 1)
        for c in range(CAP):
            hot = jnp.where(place == index[c : c + 1], 1.0, 0.0).astype(bf16)
            if hot_ref is not None:
                hot_ref[:, c * n_src : (c + 1) * n_src] = hot
            rows_ref[:, first + c, :] = dot(params, hot, ((1,), (0,)))
            chosen = jnp.where(camera == seen_by[c : c + 1], 1.0, 0.0).astype(bf16)
            cams_out[:, first + c, :] = joined(dot(cams3, chosen, ((1,), (0,))))
        return index[:CAP] > 0

    def safe(rows_ref, cams_in, live):
        row_vals = [rows_ref[row] for row in range(width)]
        row_vals[6] = jnp.where(live, row_vals[6], 1.0)
        camcols = [cams_in[row] for row in range(cams_ref.shape[1])]
        camcols[11] = jnp.where(live, camcols[11], 4.0)
        return row_vals, camcols

    live = look_up(my_view, own_s, cam_s, None, 0)
    row_vals, camcols = safe(own_s, cam_s, live)
    for index, value in enumerate(project(row_vals, camcols)):
        par_t[:CAP, index, :] = value
    par_x[...] = folded(par_t[...].reshape(8 * 16, n_src).T).reshape(par_x.shape)

    copies = exchange(n_c, cv_peer, sem_c, lambda o: par_x.at[o], par_y.at[my_c])
    par_y[my_c] = par_x[my_c]
    finish(copies)
    low_c = lax.broadcasted_iota(jnp.int32, (half_c, 128), 1) < 64
    for z in range(half_z):
        lines = par_y[:, z, :]
        other = swapped(lines)
        par_s[z] = jnp.where(low_c, lines[:half_c], other[half_c:])
        par_s[half_z + z] = jnp.where(low_c, other[:half_c], lines[half_c:])
    copies = exchange(n_z, z_peer, sem_z.at[1], lambda o: par_s.at[o], par_q.at[my_z])
    par_q[my_z] = par_s[my_z]

    finish(asking[n_c - 1 :])
    lives = [
        look_up(v, all_s, all_cam_s, hot_s.at[v], v * CAP) for v in range(n_view)
    ]
    all_live = jnp.concatenate([jnp.where(a, 1.0, 0.0) for a in lives], axis=0) > 0.5
    row_vals, camcols = safe(all_s, all_cam_s, all_live)
    finish(copies)

    turned = unfolded(par_q[...].reshape(owners // 2, 128)).T
    left = jnp.concatenate([pieces(turned[c * 16 : (c + 1) * 16]) for c in range(CAP)], axis=1)
    found = joined(dot(left, pick_s[...], ((1,), (0,))))
    for t in range(n_tiles):
        attr_s[:, t, :] = found[:, t * slots : (t + 1) * slots]

    loads[4].wait()
    loads[5].wait()
    render_tiles(
        attr_s, pos_ref, target_ref, picture_ref,
        dx_s, dy_s, exp_s, alpha_s, trans_s, color_s,
    )

    grads = jnp.concatenate([attr_s[:, t, :] for t in range(n_tiles)], axis=1)
    sums = joined(dot(pieces(grads), pick_s[...], ((1,), (1,))))
    sums = jnp.concatenate(
        [sums[:, c * owners : (c + 1) * owners] for c in range(CAP)]
        + [jnp.zeros((128 - 16 * CAP, owners), f32)],
        axis=0,
    )
    grad_s[...] = folded(sums.T).reshape(grad_s.shape)
    copies = exchange(n_z, z_peer, sem_z.at[2], lambda o: grad_s.at[o], grad_y.at[my_z])
    grad_y[my_z] = grad_s[my_z]
    finish(copies)
    low_z = lax.broadcasted_iota(jnp.int32, (half_z, 128), 1) < 64
    for c in range(half_c):
        lines = grad_y[:, c, :]
        other = swapped(lines)
        grad_x[c] = jnp.where(low_z, lines[:half_z], other[half_z:])
        grad_x[half_c + c] = jnp.where(low_z, other[:half_z], lines[half_z:])
    copies = exchange(
        n_c * n_view, cv_peer, sem_g.at[1], lambda o: grad_x.at[o], grad_u.at[my_view, my_c]
    )
    grad_u[my_view, my_c] = grad_x[my_c]
    _, pullback = jax.vjp(lambda vals: project(vals, camcols), row_vals)
    finish(copies)
    for v in range(n_view):
        turned = unfolded(grad_u[v].reshape(n_src // 2, 128)).T
        for c in range(CAP):
            cot_s[v * CAP + c] = turned[c * 16 : (c + 1) * 16]
    (grads,) = pullback([cot_s[:, index, :] for index in range(ATTRS)])
    for row, value in enumerate(grads):
        all_s[row] = value
    total = jnp.zeros((3 * width, g_dev), f32)
    for v in range(n_view):
        line = jnp.concatenate([all_s[:, v * CAP + c, :] for c in range(CAP)], axis=1)
        total = total + dot(pieces(line), hot_s[v], ((1,), (1,)))
    out_ref[...] = joined(total)


def on_device(params, lists, tile_pos, cam_index, cams, targets):
    owners = lax.axis_size("gauss")
    n_view = lax.axis_size("view")
    n_c = max(2, owners // 16)
    n_z = owners // n_c
    width, g_dev = params.shape
    n_tiles, slots = lists.shape
    half = targets.shape[2] // 2
    rows_c = cams.shape[0]
    f32, bf16 = jnp.float32, jnp.bfloat16
    vmem = pl.BlockSpec(memory_space=pltpu.VMEM)
    plane = (slots, 2 * n_tiles, half)
    shapes = [
        ((n_z, 1, slots), f32),
        ((n_z, 1, slots), f32),
        ((n_z // 4, slots), f32),
        ((n_view, n_c, n_z // 4, slots), f32),
        ((8, 16, owners), f32),
        ((n_c, n_z // 2, 128), f32),
        ((n_c, n_z // 2, 128), f32),
        ((n_z, n_c // 2, 128), f32),
        ((n_z, n_c // 2, 128), f32),
        ((width, CAP, owners), f32),
        ((rows_c, CAP, owners), f32),
        ((width, n_view * CAP, owners), f32),
        ((rows_c, n_view * CAP, owners), f32),
        ((16, n_tiles, slots), f32),
        ((n_z, n_c // 2, 128), f32),
        ((n_z, n_c // 2, 128), f32),
        ((n_c, n_z // 2, 128), f32),
        ((n_view, n_c, n_z // 2, 128), f32),
        ((n_view * CAP, 16, owners), f32),
        ((n_view, g_dev, CAP * owners), bf16),
        ((CAP * owners, n_tiles * slots), bf16),
        (plane, f32),
        (plane, f32),
        (plane, f32),
        (plane, f32),
        (plane, f32),
        ((3,) + plane, f32),
    ]
    return pl.pallas_call(
        lambda *refs: step_kernel(n_view, n_z, n_c, *refs),
        out_shape=(
            pltpu.VMEM(targets.shape, f32),
            pltpu.VMEM((width, g_dev), f32),
        ),
        in_specs=[pl.BlockSpec(memory_space=pl.ANY)] * 6,
        out_specs=(vmem, vmem),
        scratch_shapes=[
            pltpu.VMEM(params.shape, params.dtype),
            pltpu.VMEM(lists.shape, lists.dtype),
            pltpu.SMEM(tile_pos.shape, tile_pos.dtype),
            pltpu.SMEM(cam_index.shape, cam_index.dtype),
            pltpu.VMEM(cams.shape[::-1], cams.dtype),
            pltpu.VMEM(targets.shape, targets.dtype),
            pltpu.SemaphoreType.DMA((6,)),
        ]
        + [pltpu.VMEM(shape, dtype) for shape, dtype in shapes]
        + [
            pltpu.SemaphoreType.DMA((3, 2, n_z - 1)),
            pltpu.SemaphoreType.DMA((2, n_c - 1)),
            pltpu.SemaphoreType.DMA((2, 2, n_c * n_view - 1)),
        ],
        compiler_params=pltpu.CompilerParams(collective_id=0, has_side_effects=True),
    )(params, lists, tile_pos, cam_index, cams.T, targets)


def solution(mesh):
    return jax.shard_map(
        on_device,
        mesh=mesh,
        in_specs=(
            P(None, "gauss"),
            P(("gauss", "view"), None),
            P(("gauss", "view")),
            P(("gauss", "view")),
            P(),
            P(None, ("gauss", "view"), None),
        ),
        out_specs=(P(None, ("gauss", "view"), None), P(None, "gauss")),
        check_vma=False,
    )
```
